256 devices in a mesh: ctx: 32 (over z_lo, x, y), head: 8 (over z_hi, core).
Axes of the slice: x: 4, y: 4, z: 8 (z_hi: 4, z_lo: 2; z = z_hi * 2 + z_lo), core: 2. Of those that a mesh axis runs over, the one named last changes fastest.
Arguments:
- queries: bfloat16 [8192, 4096], P(('ctx', 'head')), may hold values from -4.6 to 4.6
- fresh_keys: bfloat16 [8192, 1024], P(('ctx', 'head')), may hold values from -4.6 to 4.6
- fresh_values: bfloat16 [8192, 1024], P(('ctx', 'head')), may hold values from -6 to 6
- cache_keys: bfloat16 [8192, 1024], P('ctx', 'head'), may hold values from -6 to 6
- cache_values: bfloat16 [8192, 1024], P('ctx', 'head'), may hold values from -6 to 6
- page_request: int32 [512], P('ctx'), may hold values from 0 to 2
- prompt_lengths: int32 [2], replicated, may hold values from 1 to 7168, 8192 in all
- output_weight: bfloat16 [4096, 4096], P('head'), may hold values from -0.375 to 0.375
Outputs:
- mixed: bfloat16 [8192, 4096], P(('ctx', 'head'))
The draws below stay inside these ranges and needn't reach their ends.
Inputs may be any that keep to these rules, and one draw needn't show every extreme that they name: `page_request`: value 2 marks a free page that no prompt reads.
All inputs are finite; a program needn't handle non-finite values.
Results may differ from the reference program's by a relative error of at most 0.015.
Values may be sent and summed in bfloat16 or wider, within the bound.
A program may use at most 64 MiB of HBM per device.

```python
import math
import jax
import jax.numpy as jnp
import numpy as np
from jax import lax

D = 4096
QH = 32
KVH = 8
HD = 128
PAGE = 16
REQS = 2
BLK = 256
CPAGES = 16
NEW = 8192
CACHE = 8192
N_CTX = 32


def base_entries(key, columns):
    return jnp.clip(jax.random.normal(key, (NEW, columns), jnp.float32), -4.5, 4.5)


def draw_queries(key, part):
    entries = base_entries(jax.random.fold_in(key, 1), QH * HD)
    return entries.astype(jnp.bfloat16)


def draw_fresh_keys(key, part):
    entries = base_entries(jax.random.fold_in(key, 2), KVH * HD)
    return entries.astype(jnp.bfloat16)


def touch_ends(array, rng, smallest, high):
    shape = array.shape
    spot = [jax.random.randint(jax.random.fold_in(rng, axis), (), 0, shape[axis]) for axis in range(len(shape))]
    array = array.at[tuple(spot)].set(smallest)
    longest = shape.index(max(shape))
    spot[longest] = (spot[longest] + 1) % shape[longest]
    return array.at[tuple(spot)].set(high)


def shard_levels(own_key, extent, split, smallest, top_value):
    def one(dim, parts):
        draws = jax.random.uniform(jax.random.fold_in(jax.random.fold_in(own_key, 6), dim), (parts,), jnp.float32, smallest / len(split), top_value / len(split))
        return jnp.repeat(jnp.exp(draws), extent[dim] // parts).reshape((-1,) + (1,) * (len(extent) - dim - 1))

    gain = one(*split[0])
    for cut in split[1:]:
        gain = gain * one(*cut)
    return gain


def rank_bounds(number_of, slope):
    portions = [(1 << 20) // math.isqrt(rank ** slope) + 1 for rank in range(1, number_of + 1)]
    deviation = 1 + sum(portions) // (1 << 30)
    return np.cumsum(np.array([max(1, weight // deviation) for weight in portions]))


def skewed_ids(rng, shape, amount, skew):
    listing = rank_bounds(amount, skew)
    pick = jax.random.randint(jax.random.fold_in(rng, 1), shape, 0, int(listing[amount - 1]))
    grade = jnp.searchsorted(jnp.asarray(listing, jnp.int32), pick, side="right")
    return jax.random.permutation(jax.random.fold_in(rng, 2), amount)[grade].astype(jnp.int32)


def split_up(number_of, total, reach, slope):
    weights = [(1 << 20) // math.isqrt(rank ** slope) + 1 for rank in range(2, number_of + 1)]
    rest, counts = total - reach - (number_of - 1), [1] * (number_of - 1)
    while rest > 0:
        candidates = [i for i in range(number_of - 1) if counts[i] < reach]
        pool, budget = sum([weights[i] for i in candidates]), rest
        for i in candidates:
            extra = min(reach - counts[i], max(1, budget * weights[i] // pool), rest)
            counts[i] = counts[i] + extra
            rest = rest - extra
    return np.array([reach] + counts)


def uneven_parts(stream_key, count, total, limit, slope):
    if count == 2:
        one = jax.random.randint(stream_key, (), max(1, total - limit), min(limit, total - 1) + 1)
        return jnp.stack([one, total - one])
    lengths = jnp.asarray(split_up(count, total, limit, slope), jnp.int32)
    couples = (count - 1) // 2
    donor, taker = lengths[1:1 + 2 * couples:2], lengths[2:2 + 2 * couples:2]
    margin = jnp.minimum(donor - 1, limit - taker)
    moved = jax.random.randint(jax.random.fold_in(stream_key, 1), (couples,), 0, 1 << 20) % (margin + 1)
    lengths = lengths.at[1:1 + 2 * couples:2].set(donor - moved).at[2:2 + 2 * couples:2].set(taker + moved)
    return lengths[jax.random.permutation(jax.random.fold_in(stream_key, 2), count)]


def normal_values(rng, dims, width, limit, split=(), kind=jnp.bfloat16):
    loudness = shard_levels(rng, dims, split, -0.22, 0.18) if split else 1.0
    result = jax.random.normal(rng, dims, jnp.float32) * width * loudness
    return jnp.minimum(jnp.maximum(result, -limit), limit).astype(kind)


def setup_inputs(seed: int = 0) -> dict:
    seeds = jax.random.split(jax.random.key(seed), 9)
    return {
        "queries": draw_queries(jax.random.fold_in(seeds[8], 71), 0),
        "fresh_keys": draw_fresh_keys(jax.random.fold_in(seeds[8], 71), 0),
        "fresh_values": normal_values(seeds[2], (NEW, KVH * HD), 1.0, 6.0, ((0, 256),)),
        "cache_keys": normal_values(seeds[3], (CACHE, KVH * HD), 1.0, 6.0, ((0, 32), (1, 8))),
        "cache_values": normal_values(seeds[4], (CACHE, KVH * HD), 1.0, 6.0, ((0, 32), (1, 8))),
        "page_request": touch_ends(skewed_ids(seeds[5], (CPAGES * N_CTX,), REQS + 1, 2), jax.random.fold_in(seeds[5], 3), 0, REQS).astype(jnp.int32),
        "prompt_lengths": uneven_parts(seeds[6], REQS, NEW, NEW * 7 // 8, 2).astype(jnp.int32),
        "output_weight": normal_values(seeds[7], (QH * HD, D), (QH * HD // 16) ** -0.5, 0.375, ((0, 8),)),
    }


def positions_of_rows():
    row_ids = jnp.arange(NEW, dtype=jnp.int32)
    rank_ids = row_ids // BLK
    offsets = row_ids % BLK
    half_len = BLK // 2
    pieces = jnp.where(offsets < half_len, rank_ids, 2 * N_CTX - 1 - rank_ids)
    return (pieces * half_len + offsets % half_len).astype(jnp.int32)

def request_of(position, prompt_lengths):
    ends = jnp.cumsum(prompt_lengths).astype(jnp.int32)
    return lax.optimization_barrier(jnp.sum((position[:, None] >= ends[None, :]).astype(jnp.int32), axis=1)).astype(jnp.int32)

def reference(queries, fresh_keys, fresh_values, cache_keys, cache_values, page_request, prompt_lengths, output_weight):
    position = positions_of_rows()
    query_req = request_of(position, prompt_lengths)
    key_req = jnp.concatenate([jnp.repeat(page_request, PAGE).astype(jnp.int32), query_req])
    key_pos = jnp.concatenate([jnp.full((CACHE,), -1, jnp.int32), position])
    all_keys = jnp.concatenate([cache_keys, fresh_keys]).astype(jnp.float32).reshape(CACHE + NEW, KVH, HD)
    all_values = jnp.concatenate([cache_values, fresh_values]).astype(jnp.float32).reshape(CACHE + NEW, KVH, HD)
    group_size = QH // KVH
    score_scale = 1.0 / math.sqrt(HD)
    query_block = math.gcd(NEW, 256)

    def one_block(first_row):
        query_rows = lax.dynamic_slice_in_dim(queries, first_row, query_block, 0).astype(jnp.float32)
        query_rows = query_rows.reshape(query_block, KVH, group_size, HD)
        row_pos = lax.dynamic_slice_in_dim(position, first_row, query_block, 0)
        row_req = lax.dynamic_slice_in_dim(query_req, first_row, query_block, 0)
        visible = (row_req[:, None] == key_req[None, :]) & (key_pos[None, :] <= row_pos[:, None])

        def per_head(head_id):
            query_head = lax.dynamic_index_in_dim(query_rows, head_id, 1, keepdims=False)
            key_head = lax.dynamic_index_in_dim(all_keys, head_id, 1, keepdims=False)
            value_head = lax.dynamic_index_in_dim(all_values, head_id, 1, keepdims=False)
            scores = jnp.einsum('tgd,kd->tgk', query_head, key_head, precision=lax.Precision.HIGHEST) * score_scale
            masked = jnp.where(visible[:, None, :], scores, -1e+30)
            largest = lax.optimization_barrier(jnp.max(masked, axis=-1, keepdims=True))
            weights = jnp.where(visible[:, None, :], jnp.exp(masked - largest), 0.0)
            total_sum = lax.optimization_barrier(jnp.sum(weights, axis=-1))
            probs = lax.optimization_barrier(weights.astype(jnp.bfloat16)).astype(jnp.float32)
            summed = jnp.einsum('tgk,kd->tgd', probs, value_head, precision=lax.Precision.HIGHEST)
            return summed / total_sum[..., None]
        heads_out = lax.map(per_head, jnp.arange(KVH, dtype=jnp.int32))
        heads_out = jnp.transpose(heads_out, (1, 0, 2, 3)).reshape(query_block, QH * HD)
        return heads_out.astype(jnp.bfloat16)
    starts = jnp.arange(NEW // query_block, dtype=jnp.int32) * query_block
    attended = lax.map(one_block, starts).reshape(NEW, QH * HD)
    return jnp.dot(attended, output_weight, preferred_element_type=jnp.float32).astype(jnp.bfloat16)
```

```python
import functools
import math

import jax
import jax.numpy as jnp
from jax import lax
from jax.experimental import pallas as pl
from jax.experimental.pallas import tpu as pltpu
from jax.sharding import PartitionSpec as P

HD = 128
PAGE = 16
BF = jnp.bfloat16
F32 = jnp.float32
MESH = pl.DeviceIdType.MESH
BIG = -1e30
SCALE = math.log2(math.e) / math.sqrt(HD)
CHUNKS = 4
NT = (((1,), (1,)), ((), ()))

A2A_K, A2A_V, A2A_Q = 0, 8, 16
CK1, CK2, CV1, CV2 = 32, 36, 40, 44
FK1, FK2, FV1, FV2 = 48, 52, 56, 60
PART = 64
D2D = 72
RS = 80
N_SEM = RS + 4 * CHUNKS


def dev(zlo, x, y, zhi, core):
    return (zlo * 16 + x * 4 + y, zhi * 2 + core)


def kernel(
    q_hbm, k_hbm, v_hbm, ck_hbm, cv_hbm, w_hbm, pages, lengths, out,
    qs, ks, vs, cvs, vst, rows_sc,
    qb, qaug, kc, vct, kf, vft, kaugc, kaugf,
    acc, ml, acc_s, acc_r, ml_r, w, pf, pb, d2d_r, sb, rs_r, fin,
    send, recv, loc,
):
    c = lax.axis_index("ctx")
    h = lax.axis_index("head")
    zlo, x, y = c // 16, (c // 4) % 4, c % 4
    zhi, core = h // 2, h % 2
    slot = c % 16
    my_g, my_half = zhi % 2, zhi // 2
    partner = dev(1 - zlo, x, y, zhi, core)
    sibling = dev(zlo, x, y, zhi, 1 - core)

    def rel(same_plane, dz, dc):
        zl = zlo if same_plane else 1 - zlo
        return dev(zl, x, y, (zhi + dz) % 4, (core + dc) % 2)

    def put(src, dst, idx, target):
        return pltpu.make_async_remote_copy(
            src_ref=src, dst_ref=dst, send_sem=send.at[idx], recv_sem=recv.at[idx],
            device_id=target, device_id_type=MESH,
        )

    def stage_q(i, _):
        cols = pl.ds(pl.multiple_of(i * HD, HD), HD)
        pltpu.make_async_copy(q_hbm.at[:, cols], qs.at[i], loc.at[0]).start()
        return 0

    def stage_kv(i, _):
        cols = pl.ds(pl.multiple_of(i * HD, HD), HD)
        pltpu.make_async_copy(k_hbm.at[:, cols], ks.at[i], loc.at[1]).start()
        pltpu.make_async_copy(v_hbm.at[:, cols], vs.at[i], loc.at[2]).start()
        return 0

    ck_copy = pltpu.make_async_copy(ck_hbm, kc.at[x, y, pl.ds(0, 256)], loc.at[3])
    cv_copy = pltpu.make_async_copy(cv_hbm, cvs, loc.at[4])
    ck_copy.start()
    cv_copy.start()
    lax.fori_loop(0, 8, stage_kv, 0)
    lax.fori_loop(0, 32, stage_q, 0)

    barrier = pltpu.get_barrier_semaphore()
    peers = [rel(same, dz, dc) for same in (True, False) for dz in range(4) for dc in range(2)][1:]
    peers += [dev(zlo, (x + d) % 4, y, zhi, core) for d in (1, 2, 3)]
    peers += [dev(zlo, x, (y + d) % 4, zhi, core) for d in (1, 2, 3)]
    for p in peers:
        pl.semaphore_signal(barrier, inc=1, device_id=p, device_id_type=MESH)

    lane = lax.broadcasted_iota(jnp.int32, (1, HD), 1)
    for p in range(16):
        rows_sc[p : p + 1, :] = jnp.where(lane == pages[p], 1.0, 0.0).astype(F32)
    kc[x, y, 256:272, :] = rows_sc[...].astype(BF)
    cv_copy.wait()
    vct[x, y] = cvs[...].astype(F32).T.astype(BF)
    ck_copy.wait()
    pltpu.make_async_copy(ks, ks, loc.at[1]).wait()
    pltpu.make_async_copy(vs, vs, loc.at[2]).wait()
    pltpu.make_async_copy(qs, qs, loc.at[0]).wait()

    pl.semaphore_wait(barrier, len(peers))

    copies = []

    def go(*args):
        cp = put(*args)
        cp.start()
        copies.append(cp)
        return cp

    k_in, v_in, q_in = [], [], []
    for dz in range(4):
        for dc in range(2):
            i = dz * 2 + dc
            if i == 0:
                continue
            t = ((zhi + dz) % 4) * 2 + (core + dc) % 2
            k_in.append(go(ks.at[t], kf.at[x, y, h], A2A_K + i, rel(True, dz, dc)))
            v_in.append(go(vs.at[t], vst.at[h], A2A_V + i, rel(True, dz, dc)))
    k_own = pltpu.make_async_copy(ks.at[h], kf.at[x, y, h], loc.at[1])
    v_own = pltpu.make_async_copy(vs.at[h], vst.at[h], loc.at[2])
    k_own.start()
    v_own.start()

    ck1 = [go(kc.at[x, y], kc.at[x, y], CK1 + d, dev(zlo, x, (y + d) % 4, zhi, core)) for d in (1, 3, 2)]
    cv1 = [go(vct.at[x, y], vct.at[x, y], CV1 + d, dev(zlo, (x + d) % 4, y, zhi, core)) for d in (1, 3, 2)]

    for same in (False, True):
        for dz in (1, 3, 2, 0):
            for dc in range(2):
                i = dz * 2 + dc
                if same and i == 0:
                    continue
                t = ((zhi + dz) % 4) * 2 + (core + dc) % 2
                q_in.append(
                    go(
                        qs.at[pl.ds(t * 4, 4)],
                        qb.at[0 if same else 1, my_g, my_half, :, pl.ds(core * 32, 32)],
                        A2A_Q + i + (0 if same else 8),
                        rel(same, dz, dc),
                    )
                )
    q_own = pltpu.make_async_copy(
        qs.at[pl.ds(h * 4, 4)], qb.at[0, my_g, my_half, :, pl.ds(core * 32, 32)], loc.at[0]
    )
    q_own.start()
    w_copy = pltpu.make_async_copy(w_hbm, w, loc.at[5])
    w_copy.start()

    end0 = lengths[0]
    end1 = lengths[0] + lengths[1]

    def owner(pos):
        return (pos >= end0).astype(jnp.int32) + (pos >= end1).astype(jnp.int32)

    ql = lax.broadcasted_iota(jnp.int32, (64, HD), 1)
    qi = lax.broadcasted_iota(jnp.int32, (64, HD), 0)
    for b in range(2):
        r = c if b == 0 else (1 - zlo) * 16 + slot
        for g in range(2):
            for half in range(2):
                piece = r if half == 0 else 63 - r
                req = owner(piece * 128 + g * 64 + qi)
                val = jnp.where((ql != req) & (ql < 3), BIG, 0.0).astype(BF)
                for j in range(4):
                    qaug[b, g, half, j] = val
    kl = lax.broadcasted_iota(jnp.int32, (128, HD), 1)
    ki = lax.broadcasted_iota(jnp.int32, (128, HD), 0)

    def fresh_features(s, _):
        sid = zlo * 16 + s
        for half in range(2):
            piece = sid if half == 0 else 63 - sid
            kaugf[s, half] = jnp.where(owner(piece * 128 + ki) == kl, 1.0, 0.0).astype(BF)
        return 0

    lax.fori_loop(0, 16, fresh_features, 0)

    for cp in ck1:
        cp.wait_recv()
    ck2 = [go(kc.at[x], kc.at[x], CK2 + d, dev(zlo, (x + d) % 4, y, zhi, core)) for d in (1, 3, 2)]
    for cp in cv1:
        cp.wait_recv()
    cv2 = [go(vct.at[:, y], vct.at[:, y], CV2 + d, dev(zlo, x, (y + d) % 4, zhi, core)) for d in (1, 3, 2)]

    for cp in k_in:
        cp.wait_recv()
    k_own.wait()
    fk1 = [go(kf.at[x, y], kf.at[x, y], FK1 + d, dev(zlo, x, (y + d) % 4, zhi, core)) for d in (1, 3, 2)]
    for cp in v_in:
        cp.wait_recv()
    v_own.wait()
    vt = vst[...].reshape(256, HD).astype(F32).T.astype(BF)
    vft[x, y, 0] = vt[:, :128]
    vft[x, y, 1] = vt[:, 128:]
    fv1 = [go(vft.at[x, y], vft.at[x, y], FV1 + d, dev(zlo, (x + d) % 4, y, zhi, core)) for d in (1, 3, 2)]
    for cp in fk1:
        cp.wait_recv()
    fk2 = [go(kf.at[x], kf.at[x], FK2 + d, dev(zlo, (x + d) % 4, y, zhi, core)) for d in (1, 3, 2)]
    for cp in fv1:
        cp.wait_recv()
    fv2 = [go(vft.at[:, y], vft.at[:, y], FV2 + d, dev(zlo, x, (y + d) % 4, zhi, core)) for d in (1, 3, 2)]

    acc[...] = jnp.zeros(acc.shape, F32)
    ml[:, :, :, 0] = jnp.full((2, 2, 2, 8, 256), BIG, F32)
    ml[:, :, :, 1] = jnp.zeros((2, 2, 2, 8, 256), F32)

    for cp in ck2:
        cp.wait_recv()
    for cp in cv2:
        cp.wait_recv()
    rep_r = lax.broadcasted_iota(jnp.int32, (256, 16), 0) // PAGE
    rep_c = lax.broadcasted_iota(jnp.int32, (256, 16), 1)
    rep = jnp.where(rep_r == rep_c, 1.0, 0.0).astype(BF)

    def cache_features(s, _):
        kaugc[s] = jnp.dot(rep, kc[s // 4, s % 4, 256:272, :], preferred_element_type=F32).astype(BF)
        return 0

    lax.fori_loop(0, 16, cache_features, 0)
    for cp in q_in:
        cp.wait_recv()
    q_own.wait()
    for cp in fk2 + fv2:
        cp.wait_recv()
    w_copy.wait()

    def update(b, g, half, s, v_parts):
        n = s.shape[0] // len(v_parts)
        m_old = ml[b, g, half, 0, 0:1, :]
        m_new = jnp.maximum(m_old, jnp.max(s, axis=0, keepdims=True) * SCALE)
        fade = jnp.exp2(m_old - m_new)
        p = jnp.exp2(s * SCALE - m_new)
        l_new = ml[b, g, half, 1, 0:1, :] * fade + jnp.sum(p, axis=0, keepdims=True)
        pbf = p.astype(BF)
        pv = jnp.dot(jnp.concatenate(v_parts, axis=1), pbf, preferred_element_type=F32)
        acc[b, g, half] = acc[b, g, half] * fade + pv
        ml[b, g, half, 0] = jnp.broadcast_to(m_new, (8, 256))
        ml[b, g, half, 1] = jnp.broadcast_to(l_new, (8, 256))

    def cache_tile(b, g, t):
        def score():
            k = jnp.concatenate([kc[t, :, 0:256, :].reshape(1024, HD), kaugc[pl.ds(t * 4, 4)].reshape(1024, HD)], axis=1)
            q = jnp.concatenate([qb[b, g].reshape(512, HD), qaug[b, g].reshape(512, HD)], axis=1)
            return lax.dot_general(k, q, NT, preferred_element_type=F32)

        def rest(s):
            vp = [vct[t, i] for i in range(4)]
            v = jnp.concatenate(vp, axis=1)
            m_old = jnp.concatenate([ml[b, g, 0, 0, 0:1, :], ml[b, g, 1, 0, 0:1, :]], axis=1)
            l_old = jnp.concatenate([ml[b, g, 0, 1, 0:1, :], ml[b, g, 1, 1, 0:1, :]], axis=1)
            m_new = jnp.maximum(m_old, jnp.max(s, axis=0, keepdims=True) * SCALE)
            fade = jnp.exp2(m_old - m_new)
            p = jnp.exp2(s * SCALE - m_new)
            l_new = l_old * fade + jnp.sum(p, axis=0, keepdims=True)
            pv = jnp.dot(v, p.astype(BF), preferred_element_type=F32)
            for half in range(2):
                part = slice(half * 256, half * 256 + 256)
                acc[b, g, half] = acc[b, g, half] * fade[:, part] + pv[:, part]
                ml[b, g, half, 0] = jnp.broadcast_to(m_new[:, part], (8, 256))
                ml[b, g, half, 1] = jnp.broadcast_to(l_new[:, part], (8, 256))

        return score, rest

    def fresh_tile(b, g, qhalf, t, khalf, causal):
        def score():
            k = jnp.concatenate(
                [
                    kf[pl.ds(t * 2, 2), :, pl.ds(khalf * 4, 4)].reshape(1024, HD),
                    kaugf[pl.ds(t * 8, 8), khalf].reshape(1024, HD),
                ],
                axis=1,
            )
            q = jnp.concatenate([qb[b, g, qhalf].reshape(256, HD), qaug[b, g, qhalf].reshape(256, HD)], axis=1)
            s = lax.dot_general(k, q, NT, preferred_element_type=F32)
            if causal:
                sub = lax.broadcasted_iota(jnp.int32, (1024, HD), 0)
                ln = lax.broadcasted_iota(jnp.int32, (1024, HD), 1) % 64
                sign = 1 - 2 * khalf
                gap = sign * 128 * (sub // 128) + sub % 128 - ln
                hide = gap + (sign * 128 * (t * 8 - slot) - 64 * g) > 0
                s = jnp.concatenate([jnp.where(hide, BIG, s[:, :HD]), jnp.where(hide, BIG, s[:, HD:])], axis=1)
            return s

        def rest(s):
            update(b, g, qhalf, s, [vft[t * 2 + i // 4, i % 4, khalf] for i in range(8)])

        return score, rest

    def chain(tiles):
        s = tiles[0][0]()
        for i in range(len(tiles)):
            nxt = tiles[i + 1][0]() if i + 1 < len(tiles) else None
            tiles[i][1](s)
            s = nxt

    width = w.shape[1] // CHUNKS
    part_copies = lambda g: (
        put(acc_s.at[g], acc_r.at[g], PART + g, partner),
        put(ml.at[1, g], ml_r.at[g], PART + 2 + g, partner),
    )
    d2d_copy = lambda g, j: put(
        pb.at[g, :, 1 - core, :, pl.ds(j * width, width)],
        d2d_r.at[g, :, :, pl.ds(j * width, width)],
        D2D + g * CHUNKS + j,
        sibling,
    )

    def rs_copy(g, half, j):
        o = (half * 2 + g - zhi + 4) % 4
        cols = pl.ds(j * width, width)
        return o, put(sb.at[g, half, :, cols], rs_r.at[o, :, cols], RS + o * CHUNKS + j, dev(zlo, x, y, half * 2 + g, core))

    def phase(g, _):
        chain(
            [cache_tile(1, g, t) for t in range(4)]
            + [fresh_tile(1, g, 1, t, 0, False) for t in range(2)]
            + [fresh_tile(1, g, zlo, t, zlo, False) for t in range(2)]
        )
        acc_s[g] = acc[1, g].astype(BF)
        for cp in part_copies(g):
            cp.start()
        far = slot // 8
        chain(
            [cache_tile(0, g, t) for t in range(4)]
            + [fresh_tile(0, g, 1, t, 0, False) for t in range(2)]
            + [fresh_tile(0, g, 0, 0, 0, True), fresh_tile(0, g, 1, 1, 1, True)]
            + [fresh_tile(0, g, 1 - far, far, 1 - far, True)]
        )
        for cp in part_copies(g):
            cp.wait_recv()
        halves = []
        for half in range(2):
            m_o, l_o = ml[0, g, half, 0, 0:1, :], ml[0, g, half, 1, 0:1, :]
            m_r, l_r = ml_r[g, half, 0, 0:1, :], ml_r[g, half, 1, 0:1, :]
            m_new = jnp.maximum(m_o, m_r)
            w_o, w_r = jnp.exp2(m_o - m_new), jnp.exp2(m_r - m_new)
            inv = 1.0 / (l_o * w_o + l_r * w_r)
            att = acc[0, g, half] * (w_o * inv) + acc_r[g, half].astype(F32) * (w_r * inv)
            tr = att.T.astype(BF)
            halves.append(jnp.concatenate([tr[j * 64 : j * 64 + 64] for j in range(4)], axis=1))
        a = jnp.concatenate(halves, axis=0)

        def combine(j):
            d2d_copy(g, j).wait_recv()
            cols = slice(j * width, j * width + width)
            for half in range(2):
                total = pf[half, core, :, cols] + d2d_r[g, half, :, cols].astype(F32)
                sb[g, half, :, cols] = total.astype(BF)
                o, cp = rs_copy(g, half, j)

                @pl.when(o == 0)
                def _():
                    fin[:, cols] = total

                @pl.when(o != 0)
                def _():
                    cp.start()

        for j in range(CHUNKS):
            cols = slice(j * width, j * width + width)
            y_part = jnp.dot(a, w[:, cols], preferred_element_type=F32).reshape(2, 2, 32, width)
            pf[:, :, :, cols] = y_part
            pb[g, :, :, :, cols] = y_part.astype(BF)
            d2d_copy(g, j).start()
            if j:
                combine(j - 1)
        combine(CHUNKS - 1)
        return 0

    lax.fori_loop(0, 2, phase, 0)

    for j in range(CHUNKS):
        cols = slice(j * width, j * width + width)
        total = fin[:, cols]
        for o in (1, 2, 3):
            pltpu.make_async_copy(rs_r.at[o, :, cols], rs_r.at[o, :, cols], recv.at[RS + o * CHUNKS + j]).wait()
            total = total + rs_r[o, :, cols].astype(F32)
        out[:, cols] = total.astype(BF)

    for cp in copies:
        cp.wait_send()

    def drain(g, _):
        for cp in part_copies(g):
            cp.wait_send()
        for j in range(CHUNKS):
            d2d_copy(g, j).wait_send()
            for half in range(2):
                o, cp = rs_copy(g, half, j)

                @pl.when(o != 0)
                def _():
                    cp.wait_send()

        return 0

    lax.fori_loop(0, 2, drain, 0)


def shards(queries, fresh_keys, fresh_values, cache_keys, cache_values, page_request, prompt_lengths, output_weight):
    hbm = pl.BlockSpec(memory_space=pl.ANY)
    smem = pl.BlockSpec(memory_space=pltpu.SMEM)
    vm = pltpu.VMEM
    rows, width = queries.shape
    return pl.pallas_call(
        kernel,
        out_shape=jax.ShapeDtypeStruct((rows, width), BF),
        in_specs=[hbm] * 6 + [smem] * 2,
        out_specs=pl.BlockSpec(memory_space=pltpu.VMEM),
        scratch_shapes=[
            vm((32, 32, HD), BF), vm((8, 32, HD), BF), vm((8, 32, HD), BF), vm((256, HD), BF), vm((8, 32, HD), BF),
            vm((16, HD), F32),
            vm((2, 2, 2, 4, 64, HD), BF), vm((2, 2, 2, 4, 64, HD), BF),
            vm((4, 4, 272, HD), BF), vm((4, 4, HD, 256), BF),
            vm((4, 4, 8, 32, HD), BF), vm((4, 4, 2, HD, 128), BF),
            vm((16, 256, HD), BF), vm((16, 2, 128, HD), BF),
            vm((2, 2, 2, HD, 256), F32), vm((2, 2, 2, 2, 8, 256), F32),
            vm((2, 2, HD, 256), BF), vm((2, 2, HD, 256), BF), vm((2, 2, 2, 8, 256), F32),
            vm((512, width), BF),
            vm((2, 2, 32, width), F32), vm((2, 2, 2, 32, width), BF), vm((2, 2, 32, width), BF),
            vm((2, 2, 32, width), BF), vm((4, 32, width), BF), vm((32, width), F32),
            pltpu.SemaphoreType.DMA((N_SEM,)), pltpu.SemaphoreType.DMA((N_SEM,)), pltpu.SemaphoreType.DMA((6,)),
        ],
        compiler_params=pltpu.CompilerParams(
            collective_id=0, has_side_effects=True, vmem_limit_bytes=56 * 1024 * 1024
        ),
        name="prefill_attention",
    )(queries, fresh_keys, fresh_values, cache_keys, cache_values, output_weight, page_request, prompt_lengths)


def solution(mesh):
    placed = (
        P(("ctx", "head"), None),
        P(("ctx", "head"), None),
        P(("ctx", "head"), None),
        P("ctx", "head"),
        P("ctx", "head"),
        P("ctx"),
        P(),
        P("head", None),
    )
    return jax.shard_map(
        shards, mesh=mesh, in_specs=placed, out_specs=P(("ctx", "head"), None), check_vma=False
    )
```

```python
import functools
import math

import jax
import jax.numpy as jnp
from jax import lax
from jax.experimental import pallas as pl
from jax.experimental.pallas import tpu as pltpu
from jax.sharding import PartitionSpec as P

HD = 128
PAGE = 16
BF = jnp.bfloat16
F32 = jnp.float32
MESH = pl.DeviceIdType.MESH
BIG = -1e30
SCALE = math.log2(math.e) / math.sqrt(HD)
CHUNKS = 4
NT = (((1,), (1,)), ((), ()))

A2A_K, A2A_V, A2A_Q = 0, 8, 16
CACHE, FRESH = 32, 64
PART = 96
D2D = 100
RS = D2D + 2 * CHUNKS
N_SEM = RS + 3 * CHUNKS


def dev(zlo, x, y, zhi, core):
    return (zlo * 16 + x * 4 + y, zhi * 2 + core)


def kernel(
    q_hbm, k_hbm, v_hbm, ck_hbm, cv_hbm, w_hbm, pages, lengths, out,
    qs, ks, vs, cvs, vst, rows_sc,
    qb, qaug, kvc, kvf, kaugc, kaugf,
    acc, ml, acc_s, acc_r, ml_r, w, att_s, pf, pb, d2d_r, sb, rl, rs_r, fin,
    send, recv, loc,
):
    c = lax.axis_index("ctx")
    h = lax.axis_index("head")
    zlo, x, y = c // 16, (c // 4) % 4, c % 4
    zhi, core = h // 2, h % 2
    slot = c % 16
    my_g, my_half = zhi % 2, zhi // 2
    partner = dev(1 - zlo, x, y, zhi, core)
    sibling = dev(zlo, x, y, zhi, 1 - core)

    def rel(same_plane, dz, dc):
        zl = zlo if same_plane else 1 - zlo
        return dev(zl, x, y, (zhi + dz) % 4, (core + dc) % 2)

    def put(src, dst, idx, target, out_idx=None):
        return pltpu.make_async_remote_copy(
            src_ref=src, dst_ref=dst, send_sem=send.at[idx if out_idx is None else out_idx], recv_sem=recv.at[idx],
            device_id=target, device_id_type=MESH,
        )

    def stage_q(i, _):
        cols = pl.ds(pl.multiple_of(i * HD, HD), HD)
        pltpu.make_async_copy(q_hbm.at[:, cols], qs.at[i], loc.at[0]).start()
        return 0

    def stage_kv(i, _):
        cols = pl.ds(pl.multiple_of(i * HD, HD), HD)
        pltpu.make_async_copy(k_hbm.at[:, cols], ks.at[i], loc.at[1]).start()
        pltpu.make_async_copy(v_hbm.at[:, cols], vs.at[i], loc.at[2]).start()
        return 0

    ck_copies = [
        pltpu.make_async_copy(ck_hbm.at[pl.ds(e * 128, 128)], kvc.at[e, x, y, pl.ds(0, 128)], loc.at[3 + e]) for e in range(2)
    ]
    cv_copy = pltpu.make_async_copy(cv_hbm, cvs, loc.at[5])
    cv_copy.start()
    for cp in ck_copies:
        cp.start()
    lax.fori_loop(0, 8, stage_kv, 0)
    lax.fori_loop(0, 32, stage_q, 0)

    barrier = pltpu.get_barrier_semaphore()
    peers = [rel(same, dz, dc) for same in (True, False) for dz in range(4) for dc in range(2)][1:]
    peers += [dev(zlo, (x + d) % 4, y, zhi, core) for d in (1, 2, 3)]
    peers += [dev(zlo, x, (y + d) % 4, zhi, core) for d in (1, 2, 3)]
    for p in peers:
        pl.semaphore_signal(barrier, inc=1, device_id=p, device_id_type=MESH)

    lane = lax.broadcasted_iota(jnp.int32, (1, HD), 1)
    rows_sc[...] = jnp.zeros(rows_sc.shape, F32)
    for p in range(16):
        rows_sc[p // 8, p % 8 : p % 8 + 1, :] = jnp.where(lane == pages[p], 1.0, 0.0).astype(F32)
    cv_copy.wait()
    cvt = cvs[...].astype(F32).T.astype(BF)
    for e in range(2):
        kvc[e, x, y, 128:144, :] = rows_sc[e].astype(BF)
        kvc[e, x, y, 144:272, :] = cvt[:, e * 128 : e * 128 + 128]
    for cp in ck_copies:
        cp.wait()
    pltpu.make_async_copy(ks, ks, loc.at[1]).wait()
    pltpu.make_async_copy(vs, vs, loc.at[2]).wait()
    pltpu.make_async_copy(qs, qs, loc.at[0]).wait()

    pl.semaphore_wait(barrier, len(peers))

    copies = []

    def go(*args):
        cp = put(*args)
        cp.start()
        copies.append(cp)
        return cp

    def along(e, first, d):
        if (e == 0) == first:
            return dev(zlo, x, (y + d) % 4, zhi, core)
        return dev(zlo, (x + d) % 4, y, zhi, core)

    def block(buf, e, j):
        if e == 0:
            return buf.at[e, x, (y - j + 4) % 4]
        return buf.at[e, (x - j + 4) % 4, y]

    def relayed(buf, e, d, start):
        if e == 0:
            return buf.at[e, (x - d + 4) % 4, pl.ds(start, 2)]
        return buf.at[e, pl.ds(start, 2), (y - d + 4) % 4]

    def ring_one(buf, base, e):
        b = block(buf, e, 0)
        return [go(b, b, base + e * 16 + d, along(e, True, d)) for d in (1, 3, 2)]

    def ring_two(buf, base, e, js):
        res = []
        for j in js:
            b = block(buf, e, j)
            res += [go(b, b, base + e * 16 + 4 + j * 2 + i, along(e, False, d)) for i, d in enumerate((1, 3))]
        return res

    def relay(buf, base, e):
        near = relayed(buf, e, 1, 0), relayed(buf, e, 3, 2)
        return [
            put(near[0], near[0], base + e * 16 + 12, along(e, False, 1)),
            put(near[1], near[1], base + e * 16 + 13, along(e, False, 3)),
        ]

    def begin(cps):
        for cp in cps:
            cp.start()

    def arrived(cps):
        for cp in cps:
            cp.wait_recv()

    k_in, v_in = [], []
    for dz in (1, 3, 2, 0):
        for dc in range(2):
            i = dz * 2 + dc
            if i == 0:
                continue
            t = ((zhi + dz) % 4) * 2 + (core + dc) % 2
            k_in.append(go(ks.at[t], kvf.at[my_half, x, y, pl.ds((h % 4) * 32, 32)], A2A_K + i, rel(True, dz, dc)))
            v_in.append(go(vs.at[t], vst.at[h], A2A_V + i, rel(True, dz, dc)))
    k_own = pltpu.make_async_copy(ks.at[h], kvf.at[my_half, x, y, pl.ds((h % 4) * 32, 32)], loc.at[1])
    v_own = pltpu.make_async_copy(vs.at[h], vst.at[h], loc.at[2])
    k_own.start()
    v_own.start()

    c1 = ring_one(kvc, CACHE, 0) + ring_one(kvc, CACHE, 1)
    c2 = ring_two(kvc, CACHE, 0, [0]) + ring_two(kvc, CACHE, 1, [0])

    q_in = {}
    for same in (True, False):
        q_in[same] = []
        for dz in (1, 3, 2, 0):
            for dc in range(2):
                i = dz * 2 + dc
                if same and i == 0:
                    continue
                t = ((zhi + dz) % 4) * 2 + (core + dc) % 2
                q_in[same].append(
                    go(
                        qs.at[pl.ds(t * 4, 4)],
                        qb.at[0 if same else 1, my_g, my_half, :, pl.ds(core * 32, 32)],
                        A2A_Q + i + (0 if same else 8),
                        rel(same, dz, dc),
                    )
                )
    q_own = pltpu.make_async_copy(
        qs.at[pl.ds(h * 4, 4)], qb.at[0, my_g, my_half, :, pl.ds(core * 32, 32)], loc.at[0]
    )
    q_own.start()
    w_copy = pltpu.make_async_copy(w_hbm, w, loc.at[6])
    w_copy.start()

    end0 = lengths[0]
    end1 = lengths[0] + lengths[1]

    def owner(pos):
        return (pos >= end0).astype(jnp.int32) + (pos >= end1).astype(jnp.int32)

    ql = lax.broadcasted_iota(jnp.int32, (64, HD), 1)
    qi = lax.broadcasted_iota(jnp.int32, (64, HD), 0)
    for b in range(2):
        r = c if b == 0 else (1 - zlo) * 16 + slot
        for g in range(2):
            for half in range(2):
                piece = r if half == 0 else 63 - r
                req = owner(piece * 128 + g * 64 + qi)
                val = jnp.where((ql != req) & (ql < 3), BIG, 0.0).astype(BF)
                for j in range(4):
                    qaug[b, g, half, j] = val
    acc[...] = jnp.zeros(acc.shape, F32)
    ml[:, :, :, 0] = jnp.full((2, 2, 2, 8, 256), BIG, F32)
    ml[:, :, :, 1] = jnp.zeros((2, 2, 2, 8, 256), F32)

    arrived(k_in)
    k_own.wait()
    arrived(v_in)
    v_own.wait()
    vt = vst[...].reshape(256, HD).astype(F32).T.astype(BF)
    for e in range(2):
        kvf[e, x, y, 128:256, :] = vt[:, e * 128 : e * 128 + 128]
    f1 = ring_one(kvf, FRESH, 0) + ring_one(kvf, FRESH, 1)
    arrived(c1)
    c2 += ring_two(kvc, CACHE, 0, [1, 3, 2]) + ring_two(kvc, CACHE, 1, [1, 3, 2])

    kl = lax.broadcasted_iota(jnp.int32, (128, HD), 1)
    ki = lax.broadcasted_iota(jnp.int32, (128, HD), 0)

    def fresh_features(s, _):
        sid = zlo * 16 + s
        for half in range(2):
            piece = sid if half == 0 else 63 - sid
            kaugf[s, half] = jnp.where(owner(piece * 128 + ki) == kl, 1.0, 0.0).astype(BF)
        return 0

    lax.fori_loop(0, 16, fresh_features, 0)

    rep_r = lax.broadcasted_iota(jnp.int32, (128, 16), 0) // PAGE
    rep_c = lax.broadcasted_iota(jnp.int32, (128, 16), 1)
    rep = jnp.where(rep_r == rep_c, 1.0, 0.0).astype(BF)

    def cache_features(d):
        xr, yr = (x - d + 4) % 4, (y - d + 4) % 4
        for i in range(4):
            kaugc[0, xr, i] = jnp.dot(rep, kvc[0, xr, i, 128:144, :], preferred_element_type=F32).astype(BF)
            kaugc[1, i, yr] = jnp.dot(rep, kvc[1, i, yr, 128:144, :], preferred_element_type=F32).astype(BF)

    def soft(s, m_old, l_old, v):
        m_new = jnp.maximum(m_old, jnp.max(s, axis=0, keepdims=True) * SCALE)
        fade = jnp.exp2(m_old - m_new)
        p = jnp.exp2(s * SCALE - m_new)
        l_new = l_old * fade + jnp.sum(p, axis=0, keepdims=True)
        return m_new, l_new, fade, jnp.dot(v, p.astype(BF), preferred_element_type=F32)

    def cache_tile(b, g, d):
        xr, yr = (x - d + 4) % 4, (y - d + 4) % 4

        def score():
            k = jnp.concatenate([kvc[0, xr, :, 0:128, :].reshape(512, HD), kvc[1, :, yr, 0:128, :].reshape(512, HD)], axis=0)
            f = jnp.concatenate([kaugc[0, xr].reshape(512, HD), kaugc[1, :, yr].reshape(512, HD)], axis=0)
            q = jnp.concatenate([qb[b, g].reshape(512, HD), qaug[b, g].reshape(512, HD)], axis=1)
            return lax.dot_general(jnp.concatenate([k, f], axis=1), q, NT, preferred_element_type=F32)

        def rest(s):
            v = jnp.concatenate(
                [kvc[0, xr, i, 144:272, :] for i in range(4)] + [kvc[1, i, yr, 144:272, :] for i in range(4)], axis=1
            )
            m_old = jnp.concatenate([ml[b, g, 0, 0, 0:1, :], ml[b, g, 1, 0, 0:1, :]], axis=1)
            l_old = jnp.concatenate([ml[b, g, 0, 1, 0:1, :], ml[b, g, 1, 1, 0:1, :]], axis=1)
            m_new, l_new, fade, pv = soft(s, m_old, l_old, v)
            for half in range(2):
                part = slice(half * 256, half * 256 + 256)
                acc[b, g, half] = acc[b, g, half] * fade[:, part] + pv[:, part]
                ml[b, g, half, 0] = jnp.broadcast_to(m_new[:, part], (8, 256))
                ml[b, g, half, 1] = jnp.broadcast_to(l_new[:, part], (8, 256))

        return score, rest

    def low_row(d):
        return [(0, (x - d + 4) % 4, i) for i in range(4)]

    def high_column(d):
        return [(1, i, (y - d + 4) % 4) for i in range(4)]

    def crossed(d):
        xr, yr = (x - d + 4) % 4, (y - d + 4) % 4
        return [(zlo, (1 - zlo) * xr + zlo * i, (1 - zlo) * i + zlo * yr) for i in range(4)]

    def fresh_tile(b, g, qhalf, blocks, sign):
        def score():
            k = jnp.concatenate([kvf[e, i, j, 0:128, :] for e, i, j in blocks], axis=0)
            f = jnp.concatenate([kaugf[i * 4 + j, e] for e, i, j in blocks], axis=0)
            q = jnp.concatenate([qb[b, g, qhalf].reshape(256, HD), qaug[b, g, qhalf].reshape(256, HD)], axis=1)
            s = lax.dot_general(jnp.concatenate([k, f], axis=1), q, NT, preferred_element_type=F32)
            if sign:
                gap = lax.broadcasted_iota(jnp.int32, (128, HD), 0) - lax.broadcasted_iota(jnp.int32, (128, HD), 1) % 64
                parts = []
                for n, (e, i, j) in enumerate(blocks):
                    hide = gap > 64 * g + sign * 128 * (slot - (i * 4 + j))
                    sn = s[n * 128 : n * 128 + 128]
                    parts.append(jnp.concatenate([jnp.where(hide, BIG, sn[:, :HD]), jnp.where(hide, BIG, sn[:, HD:])], axis=1))
                s = jnp.concatenate(parts, axis=0)
            return s

        def rest(s):
            v = jnp.concatenate([kvf[e, i, j, 128:256, :] for e, i, j in blocks], axis=1)
            m_new, l_new, fade, pv = soft(s, ml[b, g, qhalf, 0, 0:1, :], ml[b, g, qhalf, 1, 0:1, :], v)
            acc[b, g, qhalf] = acc[b, g, qhalf] * fade + pv
            ml[b, g, qhalf, 0] = jnp.broadcast_to(m_new, (8, 256))
            ml[b, g, qhalf, 1] = jnp.broadcast_to(l_new, (8, 256))

        return score, rest

    def partner_tiles(g, ds):
        pick = lambda f: [blk for d in ds for blk in f(d)]
        return [fresh_tile(1, g, 1, pick(low_row), 0), fresh_tile(1, g, zlo, pick(crossed), 0)]

    def own_tiles(g, ds):
        pick = lambda f: [blk for d in ds for blk in f(d)]
        return [
            fresh_tile(0, g, 1, pick(low_row), 0),
            fresh_tile(0, g, 0, pick(low_row), 1),
            fresh_tile(0, g, 1, pick(high_column), -1),
        ]

    def chain(tiles):
        s = tiles[0][0]()
        for i in range(len(tiles)):
            nxt = tiles[i + 1][0]() if i + 1 < len(tiles) else None
            tiles[i][1](s)
            s = nxt

    width = w.shape[1] // CHUNKS
    part_copies = lambda g: (
        put(acc_s.at[g], acc_r.at[g], PART + g, partner),
        put(ml.at[1, g], ml_r.at[g], PART + 2 + g, partner),
    )
    d2d_copy = lambda g, j: put(
        pb.at[g, :, :, pl.ds(j * width, width)],
        d2d_r.at[g, :, :, pl.ds(j * width, width)],
        D2D + g * CHUNKS + j,
        sibling,
    )

    def ring_role(g):
        v = (zhi - g + 4) % 4
        return v % 2, v // 2

    def rs_first(g, j):
        odd, up = ring_role(g)
        hi = j // (CHUNKS // 2)
        half = (1 - up) * (1 - odd * hi) + up * odd * hi
        target = (zhi + (2 * hi - 1) * (1 - 2 * odd) + 4) % 4
        place = (1 - odd) * 2 + odd * (1 - hi)
        cols = pl.ds(j * width, width)
        return put(
            sb.at[g, half, :, cols], rs_r.at[place, :, cols], RS + place * CHUNKS + j,
            dev(zlo, x, y, target, core), out_idx=RS + g * CHUNKS + j,
        )

    def rs_second(g, j):
        hi = j // (CHUNKS // 2)
        cols = pl.ds(j * width, width)
        return put(
            rl.at[:, cols], rs_r.at[hi, :, cols], RS + hi * CHUNKS + j,
            dev(zlo, x, y, (zhi + 2 * hi - 1 + 4) % 4, core), out_idx=RS + 2 * CHUNKS + j,
        )

    def landed(place, j):
        cols = pl.ds(j * width, width)
        ref = rs_r.at[place, :, cols]
        pltpu.make_async_copy(ref, ref, recv.at[RS + place * CHUNKS + j]).wait()

    def pass_on(g):
        odd, up = ring_role(g)

        @pl.when(odd == 1)
        def _():
            for j in (0, CHUNKS // 2, 1, CHUNKS // 2 + 1):
                hi = j // (CHUNKS // 2)
                half = up * (1 - hi) + (1 - up) * hi
                cols = slice(j * width, j * width + width)
                landed(2, j)
                rl[:, cols] = (pf[g, half, :, cols] + rs_r[2, :, cols].astype(F32)).astype(BF)
                rs_second(g, j).start()

    cache_features(0)
    arrived(c2)
    c3 = relay(kvc, CACHE, 0) + relay(kvc, CACHE, 1)
    begin(c3)
    arrived(f1)
    f2 = ring_two(kvf, FRESH, 0, [0, 1, 3, 2]) + ring_two(kvf, FRESH, 1, [0, 1, 3, 2])
    cache_features(1)
    cache_features(3)
    f3 = relay(kvf, FRESH, 0) + relay(kvf, FRESH, 1)
    near = (0, 1, 3)

    arrived(q_in[True])
    q_own.wait()
    chain([cache_tile(0, g, d) for g in range(2) for d in near])
    arrived(q_in[False])
    chain([cache_tile(1, 0, d) for d in near])
    arrived(c3)
    cache_features(2)
    chain([cache_tile(0, 0, 2), cache_tile(1, 0, 2)])
    arrived(f2)
    begin(f3)
    chain([cache_tile(1, 1, d) for d in near] + [cache_tile(0, 1, 2), cache_tile(1, 1, 2)])

    def fresh_step(g, _):
        chain(partner_tiles(g, near) + own_tiles(g, near))

        @pl.when(g == 0)
        def _():
            arrived(f3)

        chain(partner_tiles(g, (2,)))
        acc_s[g] = acc[1, g].astype(BF)
        for cp in part_copies(g):
            cp.start()
        chain(own_tiles(g, (2,)))
        return 0

    lax.fori_loop(0, 2, fresh_step, 0)
    w_copy.wait()

    def finish(g, _):
        for cp in part_copies(g):
            cp.wait_recv()
        for half in range(2):
            m_o, l_o = ml[0, g, half, 0, 0:1, :], ml[0, g, half, 1, 0:1, :]
            m_r, l_r = ml_r[g, half, 0, 0:1, :], ml_r[g, half, 1, 0:1, :]
            m_new = jnp.maximum(m_o, m_r)
            w_o, w_r = jnp.exp2(m_o - m_new), jnp.exp2(m_r - m_new)
            inv = 1.0 / (l_o * w_o + l_r * w_r)
            att = acc[0, g, half] * (w_o * inv) + acc_r[g, half].astype(F32) * (w_r * inv)
            tr = att.T.astype(BF)
            rows = jnp.concatenate([tr[j * 64 : j * 64 + 64] for j in range(4)], axis=1)
            att_s[half] = rows.reshape(2, 32, 512)
        a = jnp.concatenate([att_s[:, 1 - core].reshape(64, 512), att_s[:, core].reshape(64, 512)], axis=0)

        def combine(j):
            d2d_copy(g, j).wait_recv()
            cols = slice(j * width, j * width + width)
            odd, up = ring_role(g)
            total = pf[g, :, :, cols] + d2d_r[g, :, :, cols].astype(F32)
            sb[g, :, :, cols] = total.astype(BF)
            pf[g, :, :, cols] = total
            rs_first(g, j).start()

            @pl.when(odd == 0)
            def _():
                fin[:, cols] = pf[g, up, :, cols]

        order = (0, CHUNKS // 2, 1, CHUNKS // 2 + 1)
        for j in order:
            cols = slice(j * width, j * width + width)
            y_part = jnp.dot(a, w[:, cols], preferred_element_type=F32)
            pb[g, :, :, cols] = y_part[:64].astype(BF).reshape(2, 32, width)
            pf[g, :, :, cols] = y_part[64:].reshape(2, 32, width)
            d2d_copy(g, j).start()
        for j in order:
            combine(j)
        return 0

    lax.fori_loop(0, 2, finish, 0)

    pass_on(0)
    pass_on(1)
    for j in (0, CHUNKS // 2, 1, CHUNKS // 2 + 1):
        cols = slice(j * width, j * width + width)
        landed(0, j)
        landed(1, j)
        out[:, cols] = (fin[:, cols] + rs_r[0, :, cols].astype(F32) + rs_r[1, :, cols].astype(F32)).astype(BF)

    for cp in copies + c3 + f3:
        cp.wait_send()

    def drain(g, _):
        for cp in part_copies(g):
            cp.wait_send()
        for j in range(CHUNKS):
            d2d_copy(g, j).wait_send()
            rs_first(g, j).wait_send()
        return 0

    lax.fori_loop(0, 2, drain, 0)
    for j in range(CHUNKS):
        rs_second(0, j).wait_send()


def shards(queries, fresh_keys, fresh_values, cache_keys, cache_values, page_request, prompt_lengths, output_weight):
    hbm = pl.BlockSpec(memory_space=pl.ANY)
    smem = pl.BlockSpec(memory_space=pltpu.SMEM)
    vm = pltpu.VMEM
    rows, width = queries.shape
    return pl.pallas_call(
        kernel,
        out_shape=jax.ShapeDtypeStruct((rows, width), BF),
        in_specs=[hbm] * 6 + [smem] * 2,
        out_specs=pl.BlockSpec(memory_space=pltpu.VMEM),
        scratch_shapes=[
            vm((32, 32, HD), BF), vm((8, 32, HD), BF), vm((8, 32, HD), BF), vm((256, HD), BF), vm((8, 32, HD), BF),
            vm((2, 16, HD), F32),
            vm((2, 2, 2, 4, 64, HD), BF), vm((2, 2, 2, 4, 64, HD), BF),
            vm((2, 4, 4, 272, HD), BF), vm((2, 4, 4, 256, HD), BF),
            vm((2, 4, 4, 128, HD), BF), vm((16, 2, 128, HD), BF),
            vm((2, 2, 2, HD, 256), F32), vm((2, 2, 2, 2, 8, 256), F32),
            vm((2, 2, HD, 256), BF), vm((2, 2, HD, 256), BF), vm((2, 2, 2, 8, 256), F32),
            vm((512, width), BF),
            vm((2, 2, 32, 512), BF), vm((2, 2, 32, width), F32), vm((2, 2, 32, width), BF), vm((2, 2, 32, width), BF),
            vm((2, 2, 32, width), BF), vm((32, width), BF), vm((3, 32, width), BF), vm((32, width), F32),
            pltpu.SemaphoreType.DMA((N_SEM,)), pltpu.SemaphoreType.DMA((N_SEM,)), pltpu.SemaphoreType.DMA((7,)),
        ],
        compiler_params=pltpu.CompilerParams(
            collective_id=0, has_side_effects=True, vmem_limit_bytes=56 * 1024 * 1024
        ),
        name="prefill_attention",
    )(queries, fresh_keys, fresh_values, cache_keys, cache_values, output_weight, page_request, prompt_lengths)


def solution(mesh):
    placed = (
        P(("ctx", "head"), None),
        P(("ctx", "head"), None),
        P(("ctx", "head"), None),
        P("ctx", "head"),
        P("ctx", "head"),
        P("ctx"),
        P(),
        P("head", None),
    )
    return jax.shard_map(
        shards, mesh=mesh, in_specs=placed, out_specs=P(("ctx", "head"), None), check_vma=False
    )
```

```python
import functools
import math

import jax
import jax.numpy as jnp
from jax import lax
from jax.experimental import pallas as pl
from jax.experimental.pallas import tpu as pltpu
from jax.sharding import PartitionSpec as P

HD = 128
PAGE = 16
BF = jnp.bfloat16
F32 = jnp.float32
MESH = pl.DeviceIdType.MESH
BIG = -1e30
SCALE = math.log2(math.e) / math.sqrt(HD)
CHUNKS = 4
NT = (((1,), (1,)), ((), ()))

A2A_K, A2A_V, A2A_Q = 0, 8, 16
CACHE, FRESH = 32, 64
PART = 96
D2D = 100
RS = D2D + 2 * CHUNKS
N_SEM = RS + 3 * CHUNKS


def dev(zlo, x, y, zhi, core):
    return (zlo * 16 + x * 4 + y, zhi * 2 + core)


def kernel(
    q_hbm, k_hbm, v_hbm, ck_hbm, cv_hbm, w_hbm, pages, lengths, out,
    qs, ks, vs, cvs, vst, rows_sc,
    qb, qaug, kvc, kvf, kaugc, kaugf,
    acc, ml, acc_s, acc_r, ml_r, w, att_s, pf, pb, d2d_r, sb, rl, rs_r, fin,
    send, recv, loc,
):
    c = lax.axis_index("ctx")
    h = lax.axis_index("head")
    zlo, x, y = c // 16, (c // 4) % 4, c % 4
    zhi, core = h // 2, h % 2
    slot = c % 16
    my_g, my_half = zhi % 2, zhi // 2
    partner = dev(1 - zlo, x, y, zhi, core)
    sibling = dev(zlo, x, y, zhi, 1 - core)

    def rel(same_plane, dz, dc):
        zl = zlo if same_plane else 1 - zlo
        return dev(zl, x, y, (zhi + dz) % 4, (core + dc) % 2)

    def put(src, dst, idx, target, out_idx=None):
        return pltpu.make_async_remote_copy(
            src_ref=src, dst_ref=dst, send_sem=send.at[idx if out_idx is None else out_idx], recv_sem=recv.at[idx],
            device_id=target, device_id_type=MESH,
        )

    def stage_q(i, _):
        cols = pl.ds(pl.multiple_of(i * HD, HD), HD)
        pltpu.make_async_copy(q_hbm.at[:, cols], qs.at[i], loc.at[0]).start()
        return 0

    def stage_kv(i, _):
        cols = pl.ds(pl.multiple_of(i * HD, HD), HD)
        pltpu.make_async_copy(k_hbm.at[:, cols], ks.at[i], loc.at[1]).start()
        pltpu.make_async_copy(v_hbm.at[:, cols], vs.at[i], loc.at[2]).start()
        return 0

    ck_copies = [
        pltpu.make_async_copy(ck_hbm.at[pl.ds(e * 128, 128)], kvc.at[e, x, y, pl.ds(0, 128)], loc.at[3 + e]) for e in range(2)
    ]
    cv_copy = pltpu.make_async_copy(cv_hbm, cvs, loc.at[5])
    cv_copy.start()
    for cp in ck_copies:
        cp.start()
    lax.fori_loop(0, 8, stage_kv, 0)
    lax.fori_loop(0, 32, stage_q, 0)

    barrier = pltpu.get_barrier_semaphore()
    peers = [rel(same, dz, dc) for same in (True, False) for dz in range(4) for dc in range(2)][1:]
    peers += [dev(zlo, (x + d) % 4, y, zhi, core) for d in (1, 2, 3)]
    peers += [dev(zlo, x, (y + d) % 4, zhi, core) for d in (1, 2, 3)]
    for p in peers:
        pl.semaphore_signal(barrier, inc=1, device_id=p, device_id_type=MESH)

    lane = lax.broadcasted_iota(jnp.int32, (1, HD), 1)
    rows_sc[...] = jnp.zeros(rows_sc.shape, F32)
    for p in range(16):
        rows_sc[p // 8, p % 8 : p % 8 + 1, :] = jnp.where(lane == pages[p], 1.0, 0.0).astype(F32)
    cv_copy.wait()
    cvt = cvs[...].astype(F32).T.astype(BF)
    for e in range(2):
        kvc[e, x, y, 128:144, :] = rows_sc[e].astype(BF)
        kvc[e, x, y, 144:272, :] = cvt[:, e * 128 : e * 128 + 128]
    for cp in ck_copies:
        cp.wait()
    pltpu.make_async_copy(ks, ks, loc.at[1]).wait()
    pltpu.make_async_copy(vs, vs, loc.at[2]).wait()
    pltpu.make_async_copy(qs, qs, loc.at[0]).wait()

    pl.semaphore_wait(barrier, len(peers))

    copies = []

    def go(*args):
        cp = put(*args)
        cp.start()
        copies.append(cp)
        return cp

    def along(e, first, d):
        if (e == 0) == first:
            return dev(zlo, x, (y + d) % 4, zhi, core)
        return dev(zlo, (x + d) % 4, y, zhi, core)

    def block(buf, e, j):
        if e == 0:
            return buf.at[e, x, (y - j + 4) % 4]
        return buf.at[e, (x - j + 4) % 4, y]

    def relayed(buf, e, d, start):
        if e == 0:
            return buf.at[e, (x - d + 4) % 4, pl.ds(start, 2)]
        return buf.at[e, pl.ds(start, 2), (y - d + 4) % 4]

    def ring_one(buf, base, e):
        b = block(buf, e, 0)
        return [go(b, b, base + e * 16 + d, along(e, True, d)) for d in (1, 3, 2)]

    def ring_two(buf, base, e, js):
        res = []
        for j in js:
            b = block(buf, e, j)
            res += [go(b, b, base + e * 16 + 4 + j * 2 + i, along(e, False, d)) for i, d in enumerate((1, 3))]
        return res

    def relay(buf, base, e):
        near = relayed(buf, e, 1, 0), relayed(buf, e, 3, 2)
        return [
            put(near[0], near[0], base + e * 16 + 12, along(e, False, 1)),
            put(near[1], near[1], base + e * 16 + 13, along(e, False, 3)),
        ]

    def ring_two_split(buf, base):
        res = {}
        for up, down in ((0, 3), (1, 2), (3, 0), (2, 1)):
            for e in range(2):
                for i, j in ((0, up), (1, down)):
                    b = block(buf, e, j)
                    res[e, j, i] = go(b, b, base + e * 16 + 4 + j * 2 + i, along(e, False, 2 * i + 1))
        return res

    def relay_split(buf, base, e):
        res = []
        for i, js in ((0, (0, 1)), (1, (3, 2))):
            d = 2 * i + 1
            for n, j in enumerate(js):
                if e == 0:
                    b = buf.at[e, (x - d + 4) % 4, (y - j + 4) % 4]
                else:
                    b = buf.at[e, (x - j + 4) % 4, (y - d + 4) % 4]
                res.append(put(b, b, base + e * 16 + 12 + i * 2 + n, along(e, False, d)))
        return res

    def begin(cps):
        for cp in cps:
            cp.start()

    def arrived(cps):
        for cp in cps:
            cp.wait_recv()

    k_in, v_in = [], []
    for dz in (1, 3, 2, 0):
        for dc in range(2):
            i = dz * 2 + dc
            if i == 0:
                continue
            t = ((zhi + dz) % 4) * 2 + (core + dc) % 2
            k_in.append(go(ks.at[t], kvf.at[my_half, x, y, pl.ds((h % 4) * 32, 32)], A2A_K + i, rel(True, dz, dc)))
            v_in.append(go(vs.at[t], vst.at[h], A2A_V + i, rel(True, dz, dc)))
    k_own = pltpu.make_async_copy(ks.at[h], kvf.at[my_half, x, y, pl.ds((h % 4) * 32, 32)], loc.at[1])
    v_own = pltpu.make_async_copy(vs.at[h], vst.at[h], loc.at[2])
    k_own.start()
    v_own.start()

    c1 = ring_one(kvc, CACHE, 0) + ring_one(kvc, CACHE, 1)
    c2 = ring_two(kvc, CACHE, 0, [0]) + ring_two(kvc, CACHE, 1, [0])

    q_in = {}
    for same in (True, False):
        q_in[same] = []
        for dz in (1, 3, 2, 0):
            for dc in range(2):
                i = dz * 2 + dc
                if same and i == 0:
                    continue
                t = ((zhi + dz) % 4) * 2 + (core + dc) % 2
                q_in[same].append(
                    go(
                        qs.at[pl.ds(t * 4, 4)],
                        qb.at[0 if same else 1, my_g, my_half, :, pl.ds(core * 32, 32)],
                        A2A_Q + i + (0 if same else 8),
                        rel(same, dz, dc),
                    )
                )
    q_own = pltpu.make_async_copy(
        qs.at[pl.ds(h * 4, 4)], qb.at[0, my_g, my_half, :, pl.ds(core * 32, 32)], loc.at[0]
    )
    q_own.start()
    w_copy = pltpu.make_async_copy(w_hbm, w, loc.at[6])
    w_copy.start()

    end0 = lengths[0]
    end1 = lengths[0] + lengths[1]

    def owner(pos):
        return (pos >= end0).astype(jnp.int32) + (pos >= end1).astype(jnp.int32)

    ql = lax.broadcasted_iota(jnp.int32, (64, HD), 1)
    qi = lax.broadcasted_iota(jnp.int32, (64, HD), 0)
    for b in range(2):
        r = c if b == 0 else (1 - zlo) * 16 + slot
        for g in range(2):
            for half in range(2):
                piece = r if half == 0 else 63 - r
                req = owner(piece * 128 + g * 64 + qi)
                val = jnp.where((ql != req) & (ql < 3), BIG, 0.0).astype(BF)
                for j in range(4):
                    qaug[b, g, half, j] = val
    acc[...] = jnp.zeros(acc.shape, F32)
    ml[:, :, :, 0] = jnp.full((2, 2, 2, 8, 256), BIG, F32)
    ml[:, :, :, 1] = jnp.zeros((2, 2, 2, 8, 256), F32)

    arrived(c1)
    c2 += ring_two(kvc, CACHE, 0, [1, 3, 2]) + ring_two(kvc, CACHE, 1, [1, 3, 2])
    arrived(k_in)
    k_own.wait()
    arrived(v_in)
    v_own.wait()
    vt = vst[...].reshape(256, HD).astype(F32).T.astype(BF)
    for e in range(2):
        kvf[e, x, y, 128:256, :] = vt[:, e * 128 : e * 128 + 128]
    f1 = ring_one(kvf, FRESH, 0) + ring_one(kvf, FRESH, 1)

    kl = lax.broadcasted_iota(jnp.int32, (128, HD), 1)
    ki = lax.broadcasted_iota(jnp.int32, (128, HD), 0)

    def fresh_features(s, _):
        sid = zlo * 16 + s
        for half in range(2):
            piece = sid if half == 0 else 63 - sid
            kaugf[s, half] = jnp.where(owner(piece * 128 + ki) == kl, 1.0, 0.0).astype(BF)
        return 0

    lax.fori_loop(0, 16, fresh_features, 0)

    rep_r = lax.broadcasted_iota(jnp.int32, (128, 16), 0) // PAGE
    rep_c = lax.broadcasted_iota(jnp.int32, (128, 16), 1)
    rep = jnp.where(rep_r == rep_c, 1.0, 0.0).astype(BF)

    def cache_features(d):
        xr, yr = (x - d + 4) % 4, (y - d + 4) % 4
        for i in range(4):
            kaugc[0, xr, i] = jnp.dot(rep, kvc[0, xr, i, 128:144, :], preferred_element_type=F32).astype(BF)
            kaugc[1, i, yr] = jnp.dot(rep, kvc[1, i, yr, 128:144, :], preferred_element_type=F32).astype(BF)

    def soft(s, m_old, l_old, v):
        m_new = jnp.maximum(m_old, jnp.max(s, axis=0, keepdims=True) * SCALE)
        fade = jnp.exp2(m_old - m_new)
        p = jnp.exp2(s * SCALE - m_new)
        l_new = l_old * fade + jnp.sum(p, axis=0, keepdims=True)
        return m_new, l_new, fade, jnp.dot(v, p.astype(BF), preferred_element_type=F32)

    def update(s, v, b, lanes):
        m_old = jnp.concatenate([ml[b, g, half, 0, 0:1, :] for g, half in lanes], axis=1)
        l_old = jnp.concatenate([ml[b, g, half, 1, 0:1, :] for g, half in lanes], axis=1)
        m_new, l_new, fade, pv = soft(s, m_old, l_old, v)
        for n, (g, half) in enumerate(lanes):
            part = slice(n * 256, n * 256 + 256)
            acc[b, g, half] = acc[b, g, half] * fade[:, part] + pv[:, part]
            ml[b, g, half, 0] = jnp.broadcast_to(m_new[:, part], (8, 256))
            ml[b, g, half, 1] = jnp.broadcast_to(l_new[:, part], (8, 256))

    def cache_tile(b, g, d):
        xr, yr = (x - d + 4) % 4, (y - d + 4) % 4

        def score():
            k = jnp.concatenate([kvc[0, xr, :, 0:128, :].reshape(512, HD), kvc[1, :, yr, 0:128, :].reshape(512, HD)], axis=0)
            f = jnp.concatenate([kaugc[0, xr].reshape(512, HD), kaugc[1, :, yr].reshape(512, HD)], axis=0)
            q = jnp.concatenate([qb[b, g].reshape(512, HD), qaug[b, g].reshape(512, HD)], axis=1)
            return lax.dot_general(jnp.concatenate([k, f], axis=1), q, NT, preferred_element_type=F32)

        def rest(s):
            v = jnp.concatenate(
                [kvc[0, xr, i, 144:272, :] for i in range(4)] + [kvc[1, i, yr, 144:272, :] for i in range(4)], axis=1
            )
            update(s, v, b, [(g, 0), (g, 1)])

        return score, rest

    def low_rows(ds):
        return [(0, (x - d + 4) % 4, i) for d in ds for i in range(4)]

    def eight(e, t):
        return [(e, t * 2 + i // 4, i % 4) for i in range(8)]

    def fresh_tile(b, gs, qhalf, blocks, sign=None):
        def score():
            k = jnp.concatenate([kvf[e, i, j, 0:128, :] for e, i, j in blocks], axis=0)
            f = jnp.concatenate([kaugf[i * 4 + j, e] for e, i, j in blocks], axis=0)
            q = jnp.concatenate(
                [jnp.concatenate([r[b, g, qhalf].reshape(256, HD) for g in gs], axis=0) for r in (qb, qaug)], axis=1
            )
            s = lax.dot_general(jnp.concatenate([k, f], axis=1), q, NT, preferred_element_type=F32)
            if sign is not None:
                gap = lax.broadcasted_iota(jnp.int32, (128, HD), 0) - lax.broadcasted_iota(jnp.int32, (128, HD), 1) % 64
                parts = []
                for n, (e, i, j) in enumerate(blocks):
                    sn = s[n * 128 : n * 128 + 128]
                    hide = [gap > 64 * g + sign * 128 * (slot - (i * 4 + j)) for g in gs]
                    parts.append(
                        jnp.concatenate([jnp.where(hide[u // 2], BIG, sn[:, u * HD : u * HD + HD]) for u in range(2 * len(gs))], axis=1)
                    )
                s = jnp.concatenate(parts, axis=0)
            return s

        def rest(s):
            v = jnp.concatenate([kvf[e, i, j, 128:256, :] for e, i, j in blocks], axis=1)
            update(s, v, b, [(g, qhalf) for g in gs])

        return score, rest

    def chain(steps):
        waiting = None
        for step in steps:
            if isinstance(step, tuple):
                scores = step[0]()
                if waiting is not None:
                    waiting[0](waiting[1])
                waiting = (step[1], scores)
            else:
                step()
        waiting[0](waiting[1])

    width = w.shape[1] // CHUNKS
    part_copies = lambda g: (
        put(acc_s.at[g], acc_r.at[g], PART + g, partner),
        put(ml.at[1, g], ml_r.at[g], PART + 2 + g, partner),
    )
    d2d_copy = lambda g, j: put(
        pb.at[g, :, :, pl.ds(j * width, width)],
        d2d_r.at[g, :, :, pl.ds(j * width, width)],
        D2D + g * CHUNKS + j,
        sibling,
    )

    def ring_role(g):
        v = (zhi - g + 4) % 4
        return v % 2, v // 2

    def rs_first(g, j):
        odd, up = ring_role(g)
        hi = j // (CHUNKS // 2)
        half = (1 - up) * (1 - odd * hi) + up * odd * hi
        target = (zhi + (2 * hi - 1) * (1 - 2 * odd) + 4) % 4
        place = (1 - odd) * 2 + odd * (1 - hi)
        cols = pl.ds(j * width, width)
        return put(
            sb.at[g, half, :, cols], rs_r.at[place, :, cols], RS + place * CHUNKS + j,
            dev(zlo, x, y, target, core), out_idx=RS + g * CHUNKS + j,
        )

    def rs_second(g, j):
        hi = j // (CHUNKS // 2)
        cols = pl.ds(j * width, width)
        return put(
            rl.at[:, cols], rs_r.at[hi, :, cols], RS + hi * CHUNKS + j,
            dev(zlo, x, y, (zhi + 2 * hi - 1 + 4) % 4, core), out_idx=RS + 2 * CHUNKS + j,
        )

    def landed(place, j):
        cols = pl.ds(j * width, width)
        ref = rs_r.at[place, :, cols]
        pltpu.make_async_copy(ref, ref, recv.at[RS + place * CHUNKS + j]).wait()

    def pass_on(g):
        odd, up = ring_role(g)

        @pl.when(odd == 1)
        def _():
            for j in (0, CHUNKS // 2, 1, CHUNKS // 2 + 1):
                hi = j // (CHUNKS // 2)
                half = up * (1 - hi) + (1 - up) * hi
                cols = slice(j * width, j * width + width)
                landed(2, j)
                rl[:, cols] = (pf[g, half, :, cols] + rs_r[2, :, cols].astype(F32)).astype(BF)
                rs_second(g, j).start()

    cache_features(0)
    arrived(c2)
    c3 = relay(kvc, CACHE, 0) + relay(kvc, CACHE, 1)
    begin(c3)
    arrived(f1)
    f2 = ring_two_split(kvf, FRESH)
    cache_features(1)
    cache_features(3)
    f3 = relay_split(kvf, FRESH, 0) + relay_split(kvf, FRESH, 1)
    first = ((0, 0), (1, 0), (3, 1), (2, 1))
    f2_first = [f2[e, j, i] for j, i in first for e in range(2)]
    f2_last = [f2[e, j, 1 - i] for j, i in first for e in range(2)]
    near = (0, 1, 3)

    def partner_queries():
        arrived(q_in[False])

    def last_cache_row():
        arrived(c3)
        cache_features(2)

    def relay_fresh():
        arrived(f2_first)
        begin(f3)

    def near_fresh():
        arrived(f2_last)

    def last_fresh():
        arrived(f3)

    def finish(g):
        for cp in part_copies(g):
            cp.wait_recv()
        for half in range(2):
            m_o, l_o = ml[0, g, half, 0, 0:1, :], ml[0, g, half, 1, 0:1, :]
            m_r, l_r = ml_r[g, half, 0, 0:1, :], ml_r[g, half, 1, 0:1, :]
            m_new = jnp.maximum(m_o, m_r)
            w_o, w_r = jnp.exp2(m_o - m_new), jnp.exp2(m_r - m_new)
            inv = 1.0 / (l_o * w_o + l_r * w_r)
            att = acc[0, g, half] * (w_o * inv) + acc_r[g, half].astype(F32) * (w_r * inv)
            tr = att.T.astype(BF)
            rows = jnp.concatenate([tr[j * 64 : j * 64 + 64] for j in range(4)], axis=1)
            att_s[half] = rows.reshape(2, 32, 512)
        a = jnp.concatenate([att_s[:, 1 - core].reshape(64, 512), att_s[:, core].reshape(64, 512)], axis=0)

        def combine(j):
            d2d_copy(g, j).wait_recv()
            cols = slice(j * width, j * width + width)
            odd, up = ring_role(g)
            total = pf[g, :, :, cols] + d2d_r[g, :, :, cols].astype(F32)
            sb[g, :, :, cols] = total.astype(BF)
            pf[g, :, :, cols] = total
            rs_first(g, j).start()

            @pl.when(odd == 0)
            def _():
                fin[:, cols] = pf[g, up, :, cols]

        order = (0, CHUNKS // 2, 1, CHUNKS // 2 + 1)
        for j in order:
            cols = slice(j * width, j * width + width)
            y_part = jnp.dot(a, w[:, cols], preferred_element_type=F32)
            pb[g, :, :, cols] = y_part[:64].astype(BF).reshape(2, 32, width)
            pf[g, :, :, cols] = y_part[64:].reshape(2, 32, width)
            d2d_copy(g, j).start()
        for j in order:
            combine(j)

    def send_partials(g):
        acc_s[g] = acc[1, g].astype(BF)
        for cp in part_copies(g):
            cp.start()

    def partner_last(g):
        return (
            [fresh_tile(1, (g,), 1, low_rows((2,)))]
            + [fresh_tile(1, (g,), zlo, eight(zlo, t)) for t in range(2)]
        )

    far = slot // 8

    def own_last(g):
        return [
            fresh_tile(0, (g,), 1, low_rows((2,))),
            fresh_tile(0, (g,), 0, eight(0, 0), 1),
            fresh_tile(0, (g,), 1, eight(1, 1), -1),
            fresh_tile(0, (g,), 1 - far, eight(1 - far, far), 2 * far - 1),
        ]

    arrived(q_in[True])
    q_own.wait()
    own_a, own_b = own_last(0), own_last(1)
    chain(
        [cache_tile(0, g, d) for g in range(2) for d in near]
        + [partner_queries]
        + [cache_tile(1, 0, d) for d in near]
        + [last_cache_row, cache_tile(0, 0, 2), cache_tile(1, 0, 2), relay_fresh]
        + [cache_tile(1, 1, d) for d in near]
        + [cache_tile(0, 1, 2), cache_tile(1, 1, 2), near_fresh]
        + [fresh_tile(1, (0, 1), 1, low_rows(near)), fresh_tile(0, (0, 1), 1, low_rows(near)), last_fresh]
        + partner_last(0) + own_a[:1] + [lambda: send_partials(0)] + own_a[1:]
        + partner_last(1) + own_b[:1] + [lambda: send_partials(1), w_copy.wait, lambda: finish(0)] + own_b[1:]
    )
    finish(1)

    pass_on(0)
    pass_on(1)
    for j in (0, CHUNKS // 2, 1, CHUNKS // 2 + 1):
        cols = slice(j * width, j * width + width)
        landed(0, j)
        landed(1, j)
        out[:, cols] = (fin[:, cols] + rs_r[0, :, cols].astype(F32) + rs_r[1, :, cols].astype(F32)).astype(BF)

    for cp in copies + c3 + f3:
        cp.wait_send()

    def drain(g, _):
        for cp in part_copies(g):
            cp.wait_send()
        for j in range(CHUNKS):
            d2d_copy(g, j).wait_send()
            rs_first(g, j).wait_send()
        return 0

    lax.fori_loop(0, 2, drain, 0)
    for j in range(CHUNKS):
        rs_second(0, j).wait_send()


def shards(queries, fresh_keys, fresh_values, cache_keys, cache_values, page_request, prompt_lengths, output_weight):
    hbm = pl.BlockSpec(memory_space=pl.ANY)
    smem = pl.BlockSpec(memory_space=pltpu.SMEM)
    vm = pltpu.VMEM
    rows, width = queries.shape
    return pl.pallas_call(
        kernel,
        out_shape=jax.ShapeDtypeStruct((rows, width), BF),
        in_specs=[hbm] * 6 + [smem] * 2,
        out_specs=pl.BlockSpec(memory_space=pltpu.VMEM),
        scratch_shapes=[
            vm((32, 32, HD), BF), vm((8, 32, HD), BF), vm((8, 32, HD), BF), vm((256, HD), BF), vm((8, 32, HD), BF),
            vm((2, 16, HD), F32),
            vm((2, 2, 2, 4, 64, HD), BF), vm((2, 2, 2, 4, 64, HD), BF),
            vm((2, 4, 4, 272, HD), BF), vm((2, 4, 4, 256, HD), BF),
            vm((2, 4, 4, 128, HD), BF), vm((16, 2, 128, HD), BF),
            vm((2, 2, 2, HD, 256), F32), vm((2, 2, 2, 2, 8, 256), F32),
            vm((2, 2, HD, 256), BF), vm((2, 2, HD, 256), BF), vm((2, 2, 2, 8, 256), F32),
            vm((512, width), BF),
            vm((2, 2, 32, 512), BF), vm((2, 2, 32, width), F32), vm((2, 2, 32, width), BF), vm((2, 2, 32, width), BF),
            vm((2, 2, 32, width), BF), vm((32, width), BF), vm((3, 32, width), BF), vm((32, width), F32),
            pltpu.SemaphoreType.DMA((N_SEM,)), pltpu.SemaphoreType.DMA((N_SEM,)), pltpu.SemaphoreType.DMA((7,)),
        ],
        compiler_params=pltpu.CompilerParams(
            collective_id=0, has_side_effects=True, vmem_limit_bytes=56 * 1024 * 1024
        ),
        name="prefill_attention",
    )(queries, fresh_keys, fresh_values, cache_keys, cache_values, output_weight, page_request, prompt_lengths)


def solution(mesh):
    placed = (
        P(("ctx", "head"), None),
        P(("ctx", "head"), None),
        P(("ctx", "head"), None),
        P("ctx", "head"),
        P("ctx", "head"),
        P("ctx"),
        P(),
        P("head", None),
    )
    return jax.shard_map(
        shards, mesh=mesh, in_specs=placed, out_specs=P(("ctx", "head"), None), check_vma=False
    )
```

```python
import functools
import math

import jax
import jax.numpy as jnp
from jax import lax
from jax.experimental import pallas as pl
from jax.experimental.pallas import tpu as pltpu
from jax.sharding import PartitionSpec as P

HD = 128
PAGE = 16
BF = jnp.bfloat16
F32 = jnp.float32
MESH = pl.DeviceIdType.MESH
BIG = -1e30
SCALE = math.log2(math.e) / math.sqrt(HD)
CHUNKS = 8
ORDER = [j + i for j in range(CHUNKS // 2) for i in (0, CHUNKS // 2)]
NT = (((1,), (1,)), ((), ()))

A2A_K, A2A_V, A2A_Q = 0, 8, 16
CACHE, FRESH = 32, 64
PART = 96
D2D = 100
RS = D2D + 2 * CHUNKS
N_SEM = RS + 3 * CHUNKS


def dev(zlo, x, y, zhi, core):
    return (zlo * 16 + x * 4 + y, zhi * 2 + core)


def kernel(
    q_hbm, k_hbm, v_hbm, ck_hbm, cv_hbm, w_hbm, pages, lengths, out,
    qs, ks, vs, cvs, vst, rows_sc,
    qb, qaug, kvc, kvf, kaugc, kaugf,
    acc, ml, acc_s, acc_r, ml_r, w, att_s, pf, pb, d2d_r, sb, rl, rs_r, fin,
    send, recv, loc,
):
    c = lax.axis_index("ctx")
    h = lax.axis_index("head")
    zlo, x, y = c // 16, (c // 4) % 4, c % 4
    zhi, core = h // 2, h % 2
    slot = c % 16
    my_g, my_half = zhi % 2, zhi // 2
    partner = dev(1 - zlo, x, y, zhi, core)
    sibling = dev(zlo, x, y, zhi, 1 - core)

    def rel(same_plane, dz, dc):
        zl = zlo if same_plane else 1 - zlo
        return dev(zl, x, y, (zhi + dz) % 4, (core + dc) % 2)

    def put(src, dst, idx, target, out_idx=None):
        return pltpu.make_async_remote_copy(
            src_ref=src, dst_ref=dst, send_sem=send.at[idx if out_idx is None else out_idx], recv_sem=recv.at[idx],
            device_id=target, device_id_type=MESH,
        )

    def stage_q(i, _):
        cols = pl.ds(pl.multiple_of(i * HD, HD), HD)
        pltpu.make_async_copy(q_hbm.at[:, cols], qs.at[i], loc.at[0]).start()
        return 0

    def stage_kv(i, _):
        cols = pl.ds(pl.multiple_of(i * HD, HD), HD)
        pltpu.make_async_copy(k_hbm.at[:, cols], ks.at[i], loc.at[1]).start()
        pltpu.make_async_copy(v_hbm.at[:, cols], vs.at[i], loc.at[2]).start()
        return 0

    ck_copies = [
        pltpu.make_async_copy(ck_hbm.at[pl.ds(e * 128, 128)], kvc.at[e, x, y, pl.ds(0, 128)], loc.at[3 + e]) for e in range(2)
    ]
    cv_copy = pltpu.make_async_copy(cv_hbm, cvs, loc.at[5])
    cv_copy.start()
    for cp in ck_copies:
        cp.start()
    lax.fori_loop(0, 8, stage_kv, 0)
    lax.fori_loop(0, 32, stage_q, 0)

    barrier = pltpu.get_barrier_semaphore()
    peers = [rel(same, dz, dc) for same in (True, False) for dz in range(4) for dc in range(2)][1:]
    peers += [dev(zlo, (x + d) % 4, y, zhi, core) for d in (1, 2, 3)]
    peers += [dev(zlo, x, (y + d) % 4, zhi, core) for d in (1, 2, 3)]
    for p in peers:
        pl.semaphore_signal(barrier, inc=1, device_id=p, device_id_type=MESH)

    lane = lax.broadcasted_iota(jnp.int32, (1, HD), 1)
    rows_sc[...] = jnp.zeros(rows_sc.shape, F32)
    for p in range(16):
        rows_sc[p // 8, p % 8 : p % 8 + 1, :] = jnp.where(lane == pages[p], 1.0, 0.0).astype(F32)
    cv_copy.wait()
    cvt = cvs[...].astype(F32).T.astype(BF)
    for e in range(2):
        kvc[e, x, y, 128:144, :] = rows_sc[e].astype(BF)
        kvc[e, x, y, 144:272, :] = cvt[:, e * 128 : e * 128 + 128]
    for cp in ck_copies:
        cp.wait()
    pltpu.make_async_copy(ks, ks, loc.at[1]).wait()
    pltpu.make_async_copy(vs, vs, loc.at[2]).wait()
    pltpu.make_async_copy(qs, qs, loc.at[0]).wait()

    pl.semaphore_wait(barrier, len(peers))

    copies = []

    def go(*args):
        cp = put(*args)
        cp.start()
        copies.append(cp)
        return cp

    def along(e, first, d):
        if (e == 0) == first:
            return dev(zlo, x, (y + d) % 4, zhi, core)
        return dev(zlo, (x + d) % 4, y, zhi, core)

    def block(buf, e, j):
        if e == 0:
            return buf.at[e, x, (y - j + 4) % 4]
        return buf.at[e, (x - j + 4) % 4, y]

    def relayed(buf, e, d, start):
        if e == 0:
            return buf.at[e, (x - d + 4) % 4, pl.ds(start, 2)]
        return buf.at[e, pl.ds(start, 2), (y - d + 4) % 4]

    def ring_one(buf, base, e):
        b = block(buf, e, 0)
        return [go(b, b, base + e * 16 + d, along(e, True, d)) for d in (1, 3, 2)]

    def ring_two(buf, base, e, js):
        res = []
        for j in js:
            b = block(buf, e, j)
            res += [go(b, b, base + e * 16 + 4 + j * 2 + i, along(e, False, d)) for i, d in enumerate((1, 3))]
        return res

    def relay(buf, base, e):
        near = relayed(buf, e, 1, 0), relayed(buf, e, 3, 2)
        return [
            put(near[0], near[0], base + e * 16 + 12, along(e, False, 1)),
            put(near[1], near[1], base + e * 16 + 13, along(e, False, 3)),
        ]

    def ring_two_split(buf, base):
        res = {}
        for up, down in ((0, 3), (1, 2), (3, 0), (2, 1)):
            for e in range(2):
                for i, j in ((0, up), (1, down)):
                    b = block(buf, e, j)
                    res[e, j, i] = go(b, b, base + e * 16 + 4 + j * 2 + i, along(e, False, 2 * i + 1))
        return res

    def relay_split(buf, base, e):
        res = []
        for i, js in ((0, (0, 1)), (1, (3, 2))):
            d = 2 * i + 1
            for n, j in enumerate(js):
                if e == 0:
                    b = buf.at[e, (x - d + 4) % 4, (y - j + 4) % 4]
                else:
                    b = buf.at[e, (x - j + 4) % 4, (y - d + 4) % 4]
                res.append(put(b, b, base + e * 16 + 12 + i * 2 + n, along(e, False, d)))
        return res

    def begin(cps):
        for cp in cps:
            cp.start()

    def arrived(cps):
        for cp in cps:
            cp.wait_recv()

    k_in, v_in = [], []
    for dz in (1, 3, 2, 0):
        for dc in range(2):
            i = dz * 2 + dc
            if i == 0:
                continue
            t = ((zhi + dz) % 4) * 2 + (core + dc) % 2
            k_in.append(go(ks.at[t], kvf.at[my_half, x, y, pl.ds((h % 4) * 32, 32)], A2A_K + i, rel(True, dz, dc)))
            v_in.append(go(vs.at[t], vst.at[h], A2A_V + i, rel(True, dz, dc)))
    k_own = pltpu.make_async_copy(ks.at[h], kvf.at[my_half, x, y, pl.ds((h % 4) * 32, 32)], loc.at[1])
    v_own = pltpu.make_async_copy(vs.at[h], vst.at[h], loc.at[2])
    k_own.start()
    v_own.start()

    c1 = ring_one(kvc, CACHE, 0) + ring_one(kvc, CACHE, 1)
    c2 = ring_two(kvc, CACHE, 0, [0]) + ring_two(kvc, CACHE, 1, [0])

    q_in = {}
    for same in (True, False):
        q_in[same] = []
        for dz in (1, 3, 2, 0):
            for dc in range(2):
                i = dz * 2 + dc
                if same and i == 0:
                    continue
                t = ((zhi + dz) % 4) * 2 + (core + dc) % 2
                q_in[same].append(
                    go(
                        qs.at[pl.ds(t * 4, 4)],
                        qb.at[0 if same else 1, my_g, my_half, :, pl.ds(core * 32, 32)],
                        A2A_Q + i + (0 if same else 8),
                        rel(same, dz, dc),
                    )
                )
    q_own = pltpu.make_async_copy(
        qs.at[pl.ds(h * 4, 4)], qb.at[0, my_g, my_half, :, pl.ds(core * 32, 32)], loc.at[0]
    )
    q_own.start()
    w_copy = pltpu.make_async_copy(w_hbm, w, loc.at[6])
    w_copy.start()

    end0 = lengths[0]
    end1 = lengths[0] + lengths[1]

    def owner(pos):
        return (pos >= end0).astype(jnp.int32) + (pos >= end1).astype(jnp.int32)

    ql = lax.broadcasted_iota(jnp.int32, (64, HD), 1)
    qi = lax.broadcasted_iota(jnp.int32, (64, HD), 0)
    for b in range(2):
        r = c if b == 0 else (1 - zlo) * 16 + slot
        for g in range(2):
            for half in range(2):
                piece = r if half == 0 else 63 - r
                req = owner(piece * 128 + g * 64 + qi)
                val = jnp.where((ql != req) & (ql < 3), BIG, 0.0).astype(BF)
                for j in range(4):
                    qaug[b, g, half, j] = val
    acc[...] = jnp.zeros(acc.shape, F32)
    ml[:, :, :, 0] = jnp.full((2, 2, 2, 8, 256), BIG, F32)
    ml[:, :, :, 1] = jnp.zeros((2, 2, 2, 8, 256), F32)

    arrived(c1)
    c2 += ring_two(kvc, CACHE, 0, [1, 3, 2]) + ring_two(kvc, CACHE, 1, [1, 3, 2])
    arrived(k_in)
    k_own.wait()
    arrived(v_in)
    v_own.wait()
    vt = vst[...].reshape(256, HD).astype(F32).T.astype(BF)
    for e in range(2):
        kvf[e, x, y, 128:256, :] = vt[:, e * 128 : e * 128 + 128]
    f1 = ring_one(kvf, FRESH, 0) + ring_one(kvf, FRESH, 1)

    kl = lax.broadcasted_iota(jnp.int32, (128, HD), 1)
    ki = lax.broadcasted_iota(jnp.int32, (128, HD), 0)

    def fresh_features(s, _):
        sid = zlo * 16 + s
        for half in range(2):
            piece = sid if half == 0 else 63 - sid
            kaugf[s, half] = jnp.where(owner(piece * 128 + ki) == kl, 1.0, 0.0).astype(BF)
        return 0

    lax.fori_loop(0, 16, fresh_features, 0)

    rep_r = lax.broadcasted_iota(jnp.int32, (128, 16), 0) // PAGE
    rep_c = lax.broadcasted_iota(jnp.int32, (128, 16), 1)
    rep = jnp.where(rep_r == rep_c, 1.0, 0.0).astype(BF)

    def cache_features(d):
        xr, yr = (x - d + 4) % 4, (y - d + 4) % 4
        for i in range(4):
            kaugc[0, xr, i] = jnp.dot(rep, kvc[0, xr, i, 128:144, :], preferred_element_type=F32).astype(BF)
            kaugc[1, i, yr] = jnp.dot(rep, kvc[1, i, yr, 128:144, :], preferred_element_type=F32).astype(BF)

    def soft(s, m_old, l_old, v):
        m_new = jnp.maximum(m_old, jnp.max(s, axis=0, keepdims=True))
        fade = jnp.exp2(m_old - m_new)
        p = jnp.exp2(s - m_new)
        l_new = l_old * fade + jnp.sum(p, axis=0, keepdims=True)
        return m_new, l_new, fade, jnp.dot(v, p.astype(BF), preferred_element_type=F32)

    def update(s, v, b, lanes):
        m_old = jnp.concatenate([ml[b, g, half, 0, 0:1, :] for g, half in lanes], axis=1)
        l_old = jnp.concatenate([ml[b, g, half, 1, 0:1, :] for g, half in lanes], axis=1)
        m_new, l_new, fade, pv = soft(s, m_old, l_old, v)
        for n, (g, half) in enumerate(lanes):
            part = slice(n * 256, n * 256 + 256)
            acc[b, g, half] = acc[b, g, half] * fade[:, part] + pv[:, part]
            ml[b, g, half, 0] = jnp.broadcast_to(m_new[:, part], (8, 256))
            ml[b, g, half, 1] = jnp.broadcast_to(l_new[:, part], (8, 256))

    def cache_tile(b, g, d):
        xr, yr = (x - d + 4) % 4, (y - d + 4) % 4

        def score():
            k = jnp.concatenate([kvc[0, xr, :, 0:128, :].reshape(512, HD), kvc[1, :, yr, 0:128, :].reshape(512, HD)], axis=0)
            f = jnp.concatenate([kaugc[0, xr].reshape(512, HD), kaugc[1, :, yr].reshape(512, HD)], axis=0)
            q = jnp.concatenate([qb[b, g].reshape(512, HD), qaug[b, g].reshape(512, HD)], axis=1)
            return lax.dot_general(jnp.concatenate([k, f], axis=1), q, NT, preferred_element_type=F32)

        def rest(s):
            v = jnp.concatenate(
                [kvc[0, xr, i, 144:272, :] for i in range(4)] + [kvc[1, i, yr, 144:272, :] for i in range(4)], axis=1
            )
            update(s, v, b, [(g, 0), (g, 1)])

        return score, rest

    def low_rows(ds):
        return [(0, (x - d + 4) % 4, i) for d in ds for i in range(4)]

    def eight(e, t):
        return [(e, t * 2 + i // 4, i % 4) for i in range(8)]

    def fresh_tile(b, gs, qhalf, blocks, sign=None):
        def score():
            k = jnp.concatenate([kvf[e, i, j, 0:128, :] for e, i, j in blocks], axis=0)
            f = jnp.concatenate([kaugf[i * 4 + j, e] for e, i, j in blocks], axis=0)
            q = jnp.concatenate(
                [jnp.concatenate([r[b, g, qhalf].reshape(256, HD) for g in gs], axis=0) for r in (qb, qaug)], axis=1
            )
            s = lax.dot_general(jnp.concatenate([k, f], axis=1), q, NT, preferred_element_type=F32)
            if sign is not None:
                gap = lax.broadcasted_iota(jnp.int32, (128, HD), 0) - lax.broadcasted_iota(jnp.int32, (128, HD), 1) % 64
                parts = []
                for n, (e, i, j) in enumerate(blocks):
                    sn = s[n * 128 : n * 128 + 128]
                    hide = [gap > 64 * g + sign * 128 * (slot - (i * 4 + j)) for g in gs]
                    parts.append(
                        jnp.concatenate([jnp.where(hide[u // 2], BIG, sn[:, u * HD : u * HD + HD]) for u in range(2 * len(gs))], axis=1)
                    )
                s = jnp.concatenate(parts, axis=0)
            return s

        def rest(s):
            v = jnp.concatenate([kvf[e, i, j, 128:256, :] for e, i, j in blocks], axis=1)
            update(s, v, b, [(g, qhalf) for g in gs])

        return score, rest

    def chain(steps):
        waiting = None
        for step in steps:
            if isinstance(step, tuple):
                scores = step[0]()
                if waiting is not None:
                    waiting[0](waiting[1])
                waiting = (step[1], scores)
            else:
                step()
        waiting[0](waiting[1])

    width = w.shape[1] // CHUNKS
    part_copies = lambda g: (
        put(acc_s.at[g], acc_r.at[g], PART + g, partner),
        put(ml.at[1, g], ml_r.at[g], PART + 2 + g, partner),
    )
    d2d_copy = lambda g, j: put(
        pb.at[g, :, :, pl.ds(j * width, width)],
        d2d_r.at[g, :, :, pl.ds(j * width, width)],
        D2D + g * CHUNKS + j,
        sibling,
    )

    def ring_role(g):
        v = (zhi - g + 4) % 4
        return v % 2, v // 2

    def rs_first(g, j):
        odd, up = ring_role(g)
        hi = j // (CHUNKS // 2)
        half = (1 - up) * (1 - odd * hi) + up * odd * hi
        target = (zhi + (2 * hi - 1) * (1 - 2 * odd) + 4) % 4
        place = (1 - odd) * 2 + odd * (1 - hi)
        cols = pl.ds(j * width, width)
        return put(
            sb.at[g, half, :, cols], rs_r.at[place, :, cols], RS + place * CHUNKS + j,
            dev(zlo, x, y, target, core), out_idx=RS + g * CHUNKS + j,
        )

    def rs_second(g, j):
        hi = j // (CHUNKS // 2)
        cols = pl.ds(j * width, width)
        return put(
            rl.at[:, cols], rs_r.at[hi, :, cols], RS + hi * CHUNKS + j,
            dev(zlo, x, y, (zhi + 2 * hi - 1 + 4) % 4, core), out_idx=RS + 2 * CHUNKS + j,
        )

    def landed(place, j):
        cols = pl.ds(j * width, width)
        ref = rs_r.at[place, :, cols]
        pltpu.make_async_copy(ref, ref, recv.at[RS + place * CHUNKS + j]).wait()

    def pass_on(g):
        odd, up = ring_role(g)

        @pl.when(odd == 1)
        def _():
            for j in ORDER:
                hi = j // (CHUNKS // 2)
                half = up * (1 - hi) + (1 - up) * hi
                cols = slice(j * width, j * width + width)
                landed(2, j)
                rl[:, cols] = (pf[g, half, :, cols] + rs_r[2, :, cols].astype(F32)).astype(BF)
                rs_second(g, j).start()

    cache_features(0)
    arrived(c2)
    c3 = relay(kvc, CACHE, 0) + relay(kvc, CACHE, 1)
    begin(c3)
    arrived(f1)
    f2 = ring_two_split(kvf, FRESH)
    cache_features(1)
    cache_features(3)
    f3 = relay_split(kvf, FRESH, 0) + relay_split(kvf, FRESH, 1)
    first = ((0, 0), (1, 0), (3, 1), (2, 1))
    f2_first = [f2[e, j, i] for j, i in first for e in range(2)]
    f2_last = [f2[e, j, 1 - i] for j, i in first for e in range(2)]
    near = (0, 1, 3)

    def scale_queries(b):
        qb[b] = (qb[b].astype(F32) * SCALE).astype(BF)

    def partner_queries():
        arrived(q_in[False])
        scale_queries(1)

    def last_cache_row():
        arrived(c3)
        cache_features(2)

    def relay_fresh():
        arrived(f2_first)
        begin(f3)

    def near_fresh():
        arrived(f2_last)

    def last_fresh():
        arrived(f3)

    def finish(g):
        for cp in part_copies(g):
            cp.wait_recv()
        for half in range(2):
            m_o, l_o = ml[0, g, half, 0, 0:1, :], ml[0, g, half, 1, 0:1, :]
            m_r, l_r = ml_r[g, half, 0, 0:1, :], ml_r[g, half, 1, 0:1, :]
            m_new = jnp.maximum(m_o, m_r)
            w_o, w_r = jnp.exp2(m_o - m_new), jnp.exp2(m_r - m_new)
            inv = 1.0 / (l_o * w_o + l_r * w_r)
            att = acc[0, g, half] * (w_o * inv) + acc_r[g, half].astype(F32) * (w_r * inv)
            tr = att.T.astype(BF)
            rows = jnp.concatenate([tr[j * 64 : j * 64 + 64] for j in range(4)], axis=1)
            att_s[half] = rows.reshape(2, 32, 512)
        a = jnp.concatenate([att_s[:, 1 - core].reshape(64, 512), att_s[:, core].reshape(64, 512)], axis=0)

        def combine(j):
            d2d_copy(g, j).wait_recv()
            cols = slice(j * width, j * width + width)
            odd, up = ring_role(g)
            total = pf[g, :, :, cols] + d2d_r[g, :, :, cols].astype(F32)
            sb[g, :, :, cols] = total.astype(BF)
            pf[g, :, :, cols] = total
            rs_first(g, j).start()

            @pl.when(odd == 0)
            def _():
                fin[:, cols] = pf[g, up, :, cols]

        order = ORDER
        for j in order:
            cols = slice(j * width, j * width + width)
            y_part = jnp.dot(a, w[:, cols], preferred_element_type=F32)
            pb[g, :, :, cols] = y_part[:64].astype(BF).reshape(2, 32, width)
            pf[g, :, :, cols] = y_part[64:].reshape(2, 32, width)
            d2d_copy(g, j).start()
        for j in order:
            combine(j)

    def send_partials(g):
        acc_s[g] = acc[1, g].astype(BF)
        for cp in part_copies(g):
            cp.start()

    def partner_last(g):
        return (
            [fresh_tile(1, (g,), 1, low_rows((2,)))]
            + [fresh_tile(1, (g,), zlo, eight(zlo, t)) for t in range(2)]
        )

    far = slot // 8

    def own_last(g):
        return [
            fresh_tile(0, (g,), 1, low_rows((2,))),
            fresh_tile(0, (g,), 0, eight(0, 0), 1),
            fresh_tile(0, (g,), 1, eight(1, 1), -1),
            fresh_tile(0, (g,), 1 - far, eight(1 - far, far), 2 * far - 1),
        ]

    arrived(q_in[True])
    q_own.wait()
    scale_queries(0)
    own_a, own_b = own_last(0), own_last(1)
    chain(
        [cache_tile(0, g, d) for g in range(2) for d in near]
        + [partner_queries]
        + [cache_tile(1, 0, d) for d in near]
        + [last_cache_row, cache_tile(0, 0, 2), cache_tile(1, 0, 2), relay_fresh]
        + [cache_tile(1, 1, d) for d in near]
        + [cache_tile(0, 1, 2), cache_tile(1, 1, 2), near_fresh]
        + [fresh_tile(1, (0, 1), 1, low_rows(near)), fresh_tile(0, (0, 1), 1, low_rows(near)), last_fresh]
        + partner_last(0) + own_a[:1] + [lambda: send_partials(0)] + own_a[1:]
        + partner_last(1) + own_b[:1] + [lambda: send_partials(1), w_copy.wait, lambda: finish(0)] + own_b[1:]
    )
    finish(1)

    pass_on(0)
    pass_on(1)
    for j in ORDER:
        cols = slice(j * width, j * width + width)
        landed(0, j)
        landed(1, j)
        out[:, cols] = (fin[:, cols] + rs_r[0, :, cols].astype(F32) + rs_r[1, :, cols].astype(F32)).astype(BF)

    for cp in copies + c3 + f3:
        cp.wait_send()

    def drain(g, _):
        for cp in part_copies(g):
            cp.wait_send()
        for j in range(CHUNKS):
            d2d_copy(g, j).wait_send()
            rs_first(g, j).wait_send()
        return 0

    lax.fori_loop(0, 2, drain, 0)
    for j in range(CHUNKS):
        rs_second(0, j).wait_send()


def shards(queries, fresh_keys, fresh_values, cache_keys, cache_values, page_request, prompt_lengths, output_weight):
    hbm = pl.BlockSpec(memory_space=pl.ANY)
    smem = pl.BlockSpec(memory_space=pltpu.SMEM)
    vm = pltpu.VMEM
    rows, width = queries.shape
    return pl.pallas_call(
        kernel,
        out_shape=jax.ShapeDtypeStruct((rows, width), BF),
        in_specs=[hbm] * 6 + [smem] * 2,
        out_specs=pl.BlockSpec(memory_space=pltpu.VMEM),
        scratch_shapes=[
            vm((32, 32, HD), BF), vm((8, 32, HD), BF), vm((8, 32, HD), BF), vm((256, HD), BF), vm((8, 32, HD), BF),
            vm((2, 16, HD), F32),
            vm((2, 2, 2, 4, 64, HD), BF), vm((2, 2, 2, 4, 64, HD), BF),
            vm((2, 4, 4, 272, HD), BF), vm((2, 4, 4, 256, HD), BF),
            vm((2, 4, 4, 128, HD), BF), vm((16, 2, 128, HD), BF),
            vm((2, 2, 2, HD, 256), F32), vm((2, 2, 2, 2, 8, 256), F32),
            vm((2, 2, HD, 256), BF), vm((2, 2, HD, 256), BF), vm((2, 2, 2, 8, 256), F32),
            vm((512, width), BF),
            vm((2, 2, 32, 512), BF), vm((2, 2, 32, width), F32), vm((2, 2, 32, width), BF), vm((2, 2, 32, width), BF),
            vm((2, 2, 32, width), BF), vm((32, width), BF), vm((3, 32, width), BF), vm((32, width), F32),
            pltpu.SemaphoreType.DMA((N_SEM,)), pltpu.SemaphoreType.DMA((N_SEM,)), pltpu.SemaphoreType.DMA((7,)),
        ],
        compiler_params=pltpu.CompilerParams(
            collective_id=0, has_side_effects=True, vmem_limit_bytes=56 * 1024 * 1024
        ),
        name="prefill_attention",
    )(queries, fresh_keys, fresh_values, cache_keys, cache_values, output_weight, page_request, prompt_lengths)


def solution(mesh):
    placed = (
        P(("ctx", "head"), None),
        P(("ctx", "head"), None),
        P(("ctx", "head"), None),
        P("ctx", "head"),
        P("ctx", "head"),
        P("ctx"),
        P(),
        P("head", None),
    )
    return jax.shard_map(
        shards, mesh=mesh, in_specs=placed, out_specs=P(("ctx", "head"), None), check_vma=False
    )
```
